32 devices in a mesh: row: 8 (over z, y), col: 2 (over core), layer: 2 (over x).
Axes of the slice: x: 2, y: 2, z: 4, core: 2. Of those that a mesh axis runs over, the one named last changes fastest.
Arguments:
- matrix: float32 [1, 8, 256, 4, 2, 256], P(None, 'row', None, None, 'col'), may hold values from -8 to 113.137085, as said below
Outputs:
- factored: float32 [1, 8, 256, 4, 2, 256], P(None, 'row', None, 'layer', 'col')
The draws below stay inside these ranges and needn't reach their ends.
Inputs may be any that keep to these rules, and one draw needn't show every extreme that they name: `matrix`: viewed as in the first step it is symmetric, its leading 2 * 256 x 2 * 256 block is positive definite, and its diagonal entries lie between 2.5 and 5 times the square root of 512.
All inputs are finite; a program needn't handle non-finite values.
Results may differ from the reference program's by a relative error of at most 0.000059.
Values sent between devices are 32-bit elements; how exact they have to be, the bound alone decides.
No kernel may reach another device: no remote copies, remote signals or barrier semaphores. Data moves between devices by JAX's collectives and lax.ppermute only.
A program may use at most 128 MiB of HBM per device.

```python
import math
import jax
import jax.numpy as jnp
from jax import lax

BS = 256
RB = 1
ORDER = 2048
CB = 4
N_ROW = 8
N_COL = 2


def draw_matrix(key, part):
    first_key, second_key = jax.random.split(jax.random.fold_in(key, 17))
    base = jnp.clip(jax.random.normal(first_key, (ORDER, ORDER), jnp.float32), -5.0, 5.0)
    scales = jnp.exp(jax.random.uniform(second_key, (ORDER,), jnp.float32, math.log(2.5), math.log(5.0)))
    symmetric = (base + base.T) * 0.70710678
    rows = lax.broadcasted_iota(jnp.int32, (ORDER, ORDER), 0)
    cols = lax.broadcasted_iota(jnp.int32, (ORDER, ORDER), 1)
    whole = jnp.where(rows == cols, (scales * math.sqrt(2.0 * BS))[None, :], symmetric)
    return whole.reshape(RB, N_ROW, BS, CB, N_COL, BS)


def setup_inputs(seed: int = 0) -> dict:
    arg_keys = jax.random.split(jax.random.key(seed), 2)
    matrix = draw_matrix(jax.random.fold_in(arg_keys[1], 71), 0)
    return dict(matrix=matrix)


HIGH = lax.Precision.HIGHEST

def factor_block(diag_block):
    lower_fac = jnp.linalg.cholesky(diag_block)
    identity = jnp.eye(diag_block.shape[0], dtype=jnp.float32)
    inverse = lax.linalg.triangular_solve(lower_fac, identity, left_side=True, lower=True)
    return (lower_fac, inverse)

def product(left, right):
    return jnp.dot(left.astype(jnp.float32), right.astype(jnp.float32), precision=HIGH, preferred_element_type=jnp.float32)

def reference(matrix):
    work = matrix.reshape(ORDER, ORDER)
    lower_first, inverse_first = factor_block(work[:BS, :BS])
    panel_first = jnp.concatenate([lower_first, product(work[BS:, :BS], inverse_first.T)], axis=0)
    column_next = work[:, BS:2 * BS] - product(panel_first, panel_first[BS:2 * BS].T)
    lower_next, inverse_next = factor_block(column_next[BS:2 * BS])
    panel_next = jnp.concatenate([jnp.zeros((BS, BS), jnp.float32), lower_next, product(column_next[2 * BS:], inverse_next.T)], axis=0)
    panels = jnp.concatenate([panel_first, panel_next], axis=1)
    rest = work[:, 2 * BS:] - product(panels, panels[2 * BS:].T)
    return jnp.concatenate([panels, rest], axis=1).reshape(matrix.shape)
```

```python
import functools

import jax
import jax.numpy as jnp
from jax import lax
from jax.experimental import pallas as pl
from jax.experimental.pallas import tpu as pltpu
from jax.sharding import PartitionSpec as P

HIGH = lax.Precision.HIGHEST
F32 = jnp.float32
AXES = ("row", "col", "layer")
VMEM = pl.BlockSpec(memory_space=pltpu.VMEM)
SMEM = pl.BlockSpec(memory_space=pltpu.SMEM)
LANES = 128
SUB = 8


def contract(left, right, ldim, rdim):
    return lax.dot_general(
        left,
        right,
        (((ldim,), (rdim,)), ((), ())),
        precision=HIGH,
        preferred_element_type=F32,
    )


def nn(a, b):
    return contract(a, b, 1, 0)


def nt(a, b):
    return contract(a, b, 1, 1)


def tn(a, b):
    return contract(a, b, 0, 0)


def row_of(tile, k):
    return jnp.broadcast_to(tile[k : k + 1, :], tile.shape)


def small_inverse(block):
    size = block.shape[0]
    tiles = size // SUB
    width = 2 * size
    rows = lax.broadcasted_iota(jnp.int32, (size, size), 0)
    cols = lax.broadcasted_iota(jnp.int32, (size, size), 1)
    eye = jnp.where(rows == cols, 1.0, 0.0).astype(F32)
    full = jnp.concatenate([block, eye], axis=1)
    v = [full[SUB * t : SUB * (t + 1)] for t in range(tiles)]
    sub = lax.broadcasted_iota(jnp.int32, (SUB, width), 0)
    for s in range(tiles):
        c = {
            (j, t): jnp.broadcast_to(v[t][:, SUB * s + j : SUB * s + j + 1], (SUB, width))
            for j in range(SUB)
            for t in range(s, tiles)
        }
        pivots = jnp.ones((SUB, width), F32)
        for k in range(0, SUB, 2):
            p = row_of(c[k, s], k)
            q = row_of(c[k, s], k + 1)
            w = row_of(c[k + 1, s], k + 1)
            det = p * w - q * q
            over_det = 1.0 / det
            over_p = 1.0 / p
            v0, v1 = row_of(v[s], k), row_of(v[s], k + 1)
            c0 = {j: row_of(c[j, s], k) for j in range(k + 2, SUB)}
            c1 = {j: row_of(c[j, s], k + 1) for j in range(k + 2, SUB)}
            pivots = jnp.where(sub == k, p, jnp.where(sub == k + 1, det * over_p, pivots))
            for t in range(s, tiles):
                m0 = (w * c[k, t] - q * c[k + 1, t]) * over_det
                m1 = (p * c[k + 1, t] - q * c[k, t]) * over_det
                if t == s:
                    m0 = jnp.where(sub > k + 1, m0, jnp.where(sub == k + 1, q * over_p, 0.0))
                    m1 = jnp.where(sub > k + 1, m1, 0.0)
                v[t] = v[t] - m0 * v0 - m1 * v1
                for j in range(k + 2, SUB):
                    c[j, t] = c[j, t] - m0 * c0[j] - m1 * c1[j]
        v[s] = v[s] * lax.rsqrt(pivots)
    return jnp.concatenate(v, axis=0)[:, size:]


def inverse_factor(a, x):
    n = a.shape[0]
    base = min(n, LANES // 2)
    x[...] = jnp.zeros((n, n), F32)
    for lo in range(0, n, base):
        hi = lo + base
        inv = small_inverse(a[lo:hi, lo:hi])
        if lo:
            x[lo:hi, :lo] = nn(inv, x[lo:hi, :lo])
        x[lo:hi, lo:hi] = inv
        if hi < n:
            upper = nn(inv, a[lo:hi, hi:])
            a[hi:, hi:] = a[hi:, hi:] - tn(upper, upper)
            x[hi:, :hi] = x[hi:, :hi] - tn(upper, x[lo:hi, :hi])


def first_kernel(row, w00, w01, inv, q, a):
    @pl.when(row[0] == 0)
    def _():
        a[...] = w00[...]
        inverse_factor(a, inv)
        q[...] = nn(inv[...], w01[...])


def second_kernel(row, w11, q, inv, a):
    @pl.when(row[0] == 0)
    def _():
        a[...] = w11[...] - tn(q[...], q[...])
        inverse_factor(a, inv)


def call_first(row, w00, w01):
    n = w00.shape[0]
    block = jax.ShapeDtypeStruct((n, n), F32)
    return pl.pallas_call(
        first_kernel,
        out_shape=(block, block),
        in_specs=[SMEM, VMEM, VMEM],
        out_specs=(VMEM, VMEM),
        scratch_shapes=[pltpu.VMEM((n, n), F32)],
    )(row, w00, w01)


def call_second(row, w11, q):
    n = w11.shape[0]
    return pl.pallas_call(
        second_kernel,
        out_shape=jax.ShapeDtypeStruct((n, n), F32),
        in_specs=[SMEM, VMEM, VMEM],
        out_specs=VMEM,
        scratch_shapes=[pltpu.VMEM((n, n), F32)],
    )(row, w11, q)


def lower_part(x):
    rows = lax.broadcasted_iota(jnp.int32, x.shape, 0)
    cols = lax.broadcasted_iota(jnp.int32, x.shape, 1)
    return jnp.where(rows >= cols, x, 0.0)


def early_kernel(row, wr, tile, wg, inv0, q, p0, t1r, t1g, acc):
    step = pl.program_id(0)

    @pl.when(step == 0)
    def _():
        solved = nt(wr[0], inv0[...])
        solved = jnp.where(row[0] == 0, lower_part(solved), solved)
        p0[...] = solved
        t1r[...] = wr[1] - nn(solved, q[...])

    first, second = wg[0, 0], wg[0, 1]
    p0g = nt(first, inv0[...])
    t1g[0] = second - nn(p0g, q[...])
    acc[0] = tile[0] - nt(p0[...], p0g)


def late_kernel(ids, p0, t1r, t1g, acc, inv1, out, p1):
    step = pl.program_id(0)

    @pl.when(step == 0)
    def _():
        solved = nt(t1r[...], inv1[...])
        solved = jnp.where(ids[0] == 1, lower_part(solved), solved)
        p1[...] = jnp.where(ids[0] == 0, 0.0, solved)

    p1g = nt(t1g[0], inv1[...])
    rest = acc[0] - nt(p1[...], p1g)
    block = ids[1] + step * ids[2]
    out[0] = jnp.where(block == 0, p0[...], jnp.where(block == 1, p1[...], rest))


def whole_spec(shape):
    return pl.BlockSpec(shape, lambda i: (0,) * len(shape))


def step_spec(shape):
    return pl.BlockSpec((1,) + shape, lambda i: (i,) + (0,) * len(shape))


def call_early(row, wr, tiles, wg, inv0, q):
    count, n, _ = tiles.shape
    block = jax.ShapeDtypeStruct((n, n), F32)
    stack = jax.ShapeDtypeStruct((count, n, n), F32)
    return pl.pallas_call(
        early_kernel,
        grid=(count,),
        out_shape=(block, block, stack, stack),
        in_specs=[
            SMEM,
            whole_spec((2, n, n)),
            step_spec((n, n)),
            step_spec((2, n, n)),
            whole_spec((n, n)),
            whole_spec((n, n)),
        ],
        out_specs=(whole_spec((n, n)), whole_spec((n, n)), step_spec((n, n)), step_spec((n, n))),
    )(row, wr, tiles, wg, inv0, q)


def call_late(ids, p0, t1r, t1g, acc, inv1):
    count, n, _ = acc.shape
    return pl.pallas_call(
        late_kernel,
        grid=(count,),
        out_shape=jax.ShapeDtypeStruct((count, n, n), F32),
        in_specs=[
            SMEM,
            whole_spec((n, n)),
            whole_spec((n, n)),
            step_spec((n, n)),
            step_spec((n, n)),
            whole_spec((n, n)),
        ],
        out_specs=step_spec((n, n)),
        scratch_shapes=[pltpu.VMEM((n, n), F32)],
    )(ids, p0, t1r, t1g, acc, inv1)


def rounds_of(edges):
    rounds = []
    for source, target in edges:
        for taken in rounds:
            if all(source != s and target != t for s, t in taken):
                taken.append((source, target))
                break
        else:
            rounds.append([(source, target)])
    return rounds


def spread(x, row, row_total):
    gap = row_total // 2
    while gap:
        pairs = [(r, r + gap) for r in range(0, row_total, 2 * gap)]
        got = lax.ppermute(x, "row", pairs)
        x = jnp.where(row % (2 * gap) == gap, got, x)
        gap //= 2
    return x


def on_device(matrix):
    row_total = lax.axis_size("row")
    col_total = lax.axis_size("col")
    layer_total = lax.axis_size("layer")
    row = lax.axis_index("row")
    col = lax.axis_index("col")
    layer = lax.axis_index("layer")
    n = matrix.shape[2]
    col_blocks = matrix.shape[3]
    owned = col_blocks // layer_total
    levels = row_total // 2
    near = levels // layer_total
    half = n // 2
    swap = [(0, 1), (1, 0)]
    rowid = row[None].astype(jnp.int32)

    def device(r, c, l):
        return (r * col_total + c) * layer_total + l

    def permute(x, triples):
        return lax.ppermute(
            x,
            AXES,
            [(device(a, c, l), device(b, c, l)) for a, b, l in triples for c in range(col_total)],
        )

    tile = matrix.reshape(n, col_blocks, n)
    mine = tile[:, 0]
    other = lax.ppermute(mine, "col", swap)
    wr = jnp.where(col == 0, jnp.stack([mine, other]), jnp.stack([other, mine]))

    edges = []
    for l in range(layer_total):
        for gap in range(1, levels):
            for h in range(max(1, l * near), (l + 1) * near):
                for target in (h + gap, h - gap):
                    if 1 <= target < levels:
                        edges.append(((h, l), (target, l)))
    rounds = rounds_of(edges)
    level = row // 2
    got = []
    for taken in rounds:
        triples = [(2 * s + y, 2 * t + y, l) for (s, l), (t, _) in taken for y in range(2)]
        got.append(permute(mine, triples))
    pieces = jnp.stack(got + [mine])
    table = []
    for l in range(layer_total):
        for t in range(levels):
            line = []
            for h in range(l * near, (l + 1) * near):
                slot = len(rounds)
                for i, taken in enumerate(rounds):
                    if ((h, l), (t, l)) in taken:
                        slot = i
                line.append(slot)
            table.append(line)
    slots = jnp.array(table, jnp.int32)[layer * levels + level]
    held = jnp.take(pieces, slots, axis=0)
    own_tiles = lax.dynamic_slice_in_dim(tile, layer * owned, owned, 1).transpose(1, 0, 2)

    w11 = permute(wr[1], [(1, 0, l) for l in range(layer_total)])

    inv0, q = call_first(rowid, wr[0], wr[1])

    first = spread(jnp.where(col == 0, inv0, q), row, row_total)
    second = lax.ppermute(first, "col", swap)
    inv1 = call_second(rowid, w11, q)

    send = jnp.where(row == 0, own_tiles, held) if near == owned else None
    pair = permute(send, [(r, r ^ 1, l) for r in range(row_total) for l in range(layer_total)])
    even = jnp.where(row % 2 == 0, held, pair)
    odd = jnp.where(row % 2 == 0, pair, held)
    keep = jnp.where(col == 0, even, odd)
    give = jnp.where(col == 0, odd, even)
    taken = lax.ppermute(give, "col", swap)
    wg = jnp.where(col == 0, jnp.stack([keep, taken], 1), jnp.stack([taken, keep], 1))
    top = jnp.where(row == 0, own_tiles, pair)
    bottom = jnp.where(row == 0, 0.0, own_tiles)
    flipped = jnp.stack([top, bottom], 1).transpose(0, 1, 3, 2)
    wg = jnp.where(row < 2, flipped, wg)

    inv0_all = jnp.where(col == 0, first, second)
    q_all = jnp.where(col == 0, second, first)
    p0, t1r, t1g, acc = call_early(rowid, wr, own_tiles, wg, inv0_all, q_all)

    part = jnp.where(col == 0, inv1[:half], inv1[half:])
    part = spread(part, row, row_total)
    rest = lax.ppermute(part, "col", swap)
    inv1_all = jnp.where(
        col == 0, jnp.concatenate([part, rest]), jnp.concatenate([rest, part])
    )
    start = layer * owned * col_total + col
    ids = jnp.stack([row, start, jnp.full_like(row, col_total)]).astype(jnp.int32)
    out = call_late(ids, p0, t1r, t1g, acc, inv1_all)
    return out.transpose(1, 0, 2).reshape(1, 1, n, owned, 1, n)


def solution(mesh):
    in_specs = (P(None, "row", None, None, "col", None),)
    out_specs = P(None, "row", None, "layer", "col", None)
    return jax.shard_map(
        on_device, mesh=mesh, in_specs=in_specs, out_specs=out_specs, check_vma=False
    )
```

```python
import functools

import jax
import jax.numpy as jnp
from jax import lax
from jax.experimental import pallas as pl
from jax.experimental.pallas import tpu as pltpu
from jax.sharding import PartitionSpec as P

HIGH = lax.Precision.HIGHEST
F32 = jnp.float32
AXES = ("row", "col", "layer")
VMEM = pl.BlockSpec(memory_space=pltpu.VMEM)
SMEM = pl.BlockSpec(memory_space=pltpu.SMEM)
ANY = pl.BlockSpec(memory_space=pl.ANY)
LANES = 128
SUB = 8


def contract(left, right, ldim, rdim):
    return lax.dot_general(
        left,
        right,
        (((ldim,), (rdim,)), ((), ())),
        precision=HIGH,
        preferred_element_type=F32,
    )


def nn(a, b):
    return contract(a, b, 1, 0)


def nt(a, b):
    return contract(a, b, 1, 1)


def tn(a, b):
    return contract(a, b, 0, 0)


def row_of(tile, k):
    return jnp.broadcast_to(tile[k : k + 1, :], tile.shape)


def small_inverse(block):
    size = block.shape[0]
    tiles = size // SUB
    width = 2 * size
    rows = lax.broadcasted_iota(jnp.int32, (size, size), 0)
    cols = lax.broadcasted_iota(jnp.int32, (size, size), 1)
    eye = jnp.where(rows == cols, 1.0, 0.0).astype(F32)
    full = jnp.concatenate([block, eye], axis=1)
    v = [full[SUB * t : SUB * (t + 1)] for t in range(tiles)]
    sub = lax.broadcasted_iota(jnp.int32, (SUB, width), 0)
    for s in range(tiles):
        c = {
            (j, t): jnp.broadcast_to(v[t][:, SUB * s + j : SUB * s + j + 1], (SUB, width))
            for j in range(SUB)
            for t in range(s, tiles)
        }
        pivots = jnp.ones((SUB, width), F32)
        for k in range(0, SUB, 2):
            p = row_of(c[k, s], k)
            q = row_of(c[k, s], k + 1)
            w = row_of(c[k + 1, s], k + 1)
            det = p * w - q * q
            over_det = 1.0 / det
            over_p = 1.0 / p
            v0, v1 = row_of(v[s], k), row_of(v[s], k + 1)
            c0 = {j: row_of(c[j, s], k) for j in range(k + 2, SUB)}
            c1 = {j: row_of(c[j, s], k + 1) for j in range(k + 2, SUB)}
            pivots = jnp.where(sub == k, p, jnp.where(sub == k + 1, det * over_p, pivots))
            for t in range(s, tiles):
                m0 = (w * c[k, t] - q * c[k + 1, t]) * over_det
                m1 = (p * c[k + 1, t] - q * c[k, t]) * over_det
                if t == s:
                    m0 = jnp.where(sub > k + 1, m0, jnp.where(sub == k + 1, q * over_p, 0.0))
                    m1 = jnp.where(sub > k + 1, m1, 0.0)
                v[t] = v[t] - m0 * v0 - m1 * v1
                for j in range(k + 2, SUB):
                    c[j, t] = c[j, t] - m0 * c0[j] - m1 * c1[j]
        v[s] = v[s] * lax.rsqrt(pivots)
    return jnp.concatenate(v, axis=0)[:, size:]


def inverse_factor(a, x):
    n = a.shape[0]
    base = min(n, LANES // 2)
    x[...] = jnp.zeros((n, n), F32)
    for lo in range(0, n, base):
        hi = lo + base
        inv = small_inverse(a[lo:hi, lo:hi])
        if lo:
            x[lo:hi, :lo] = nn(inv, x[lo:hi, :lo])
        x[lo:hi, lo:hi] = inv
        if hi < n:
            upper = nn(inv, a[lo:hi, hi:])
            a[hi:, hi:] = a[hi:, hi:] - tn(upper, upper)
            x[hi:, :hi] = x[hi:, :hi] - tn(upper, x[lo:hi, :hi])


def split(x):
    high = x.astype(jnp.bfloat16)
    return high, (x - high.astype(F32)).astype(jnp.bfloat16)


def three(left, right, ldim, rdim):
    def part(a, b):
        return lax.dot_general(
            a, b, (((ldim,), (rdim,)), ((), ())), preferred_element_type=F32
        )

    return part(left[0], right[0]) + (part(left[0], right[1]) + part(left[1], right[0]))


def lower_part(x):
    rows = lax.broadcasted_iota(jnp.int32, x.shape, 0)
    cols = lax.broadcasted_iota(jnp.int32, x.shape, 1)
    return jnp.where(rows >= cols, x, 0.0)


def place():
    return lax.axis_index("row"), lax.axis_index("col"), lax.axis_index("layer")


def is_owner():
    row, col, _ = place()
    return (row == 0) & (col == 0)


def move(source, target, sem):
    copy = pltpu.make_async_copy(source, target, sem)
    copy.start()
    copy.wait()


def first_kernel(matrix, inv, a, x, sem):
    @pl.when(is_owner())
    def _():
        move(matrix.at[0, 0, :, 0, 0, :], a, sem.at[0])
        inverse_factor(a, x)
        move(x, inv, sem.at[0])


def second_kernel(inv0, w01, w11, inv1, a, x, b, sem):
    @pl.when(is_owner())
    def _():
        one = pltpu.make_async_copy(inv0, x, sem.at[0])
        two = pltpu.make_async_copy(w01, b, sem.at[1])
        three_ = pltpu.make_async_copy(w11, a, sem.at[2])
        one.start()
        two.start()
        three_.start()
        one.wait()
        two.wait()
        three_.wait()
        q = nn(x[...], b[...])
        a[...] = a[...] - tn(q, q)
        inverse_factor(a, x)
        move(x, inv1, sem.at[0])


def factor_cost(n):
    return pl.CostEstimate(flops=40 * n**3, transcendentals=0, bytes_accessed=64 * n * n * 4)


def call_first(matrix, n):
    return pl.pallas_call(
        first_kernel,
        out_shape=jax.ShapeDtypeStruct((n, n), F32),
        in_specs=[ANY],
        out_specs=ANY,
        scratch_shapes=[pltpu.VMEM((n, n), F32)] * 2 + [pltpu.SemaphoreType.DMA((1,))],
        cost_estimate=factor_cost(n),
        name="first",
    )(matrix)


def call_second(inv0, w01, w11):
    n = w11.shape[0]
    return pl.pallas_call(
        second_kernel,
        out_shape=jax.ShapeDtypeStruct((n, n), F32),
        in_specs=[ANY] * 3,
        out_specs=ANY,
        scratch_shapes=[pltpu.VMEM((n, n), F32)] * 3 + [pltpu.SemaphoreType.DMA((3,))],
        cost_estimate=factor_cost(n),
        name="second",
    )(inv0, w01, w11)


def early_kernel(dims, table, matrix, *refs):
    count, owned, near, levels = dims
    own, sib = refs[:count], refs[count : 2 * count]
    inv_own, inv_sib = refs[2 * count : 2 * count + 2]
    p0, t1r, t1g, acc = refs[2 * count + 2 : 2 * count + 6]
    inv, w01, wr, wg, tiles, sem, sems = refs[2 * count + 6 :]
    row, col, layer = place()
    level, odd = row // 2, row % 2

    def fetch(slot, from_own, target, s):
        for i in range(count):

            @pl.when((slot == i) & from_own)
            def _():
                pltpu.make_async_copy(own[i], target, s).start()

            @pl.when((slot == i) & jnp.logical_not(from_own))
            def _():
                pltpu.make_async_copy(sib[i], target, s).start()

    def wait(target, s):
        pltpu.make_async_copy(own[0], target, s).wait()

    @pl.when(col == 0)
    def _():
        pltpu.make_async_copy(inv_own, inv, sem.at[0]).start()

    @pl.when(col != 0)
    def _():
        pltpu.make_async_copy(inv_sib, inv, sem.at[0]).start()

    line = (layer * levels + level) * (2 * near + 1)
    fetch(table[line + 2 * near], col != odd, w01, sem.at[1])
    pltpu.make_async_copy(own[0], wr.at[col], sem.at[2]).start()
    pltpu.make_async_copy(sib[0], wr.at[1 - col], sem.at[3]).start()

    def start(k, _):
        pltpu.make_async_copy(
            matrix.at[0, 0, :, layer * owned + k, 0, :], tiles.at[k], sems.at[0, k]
        ).start()
        slot = jnp.where((odd == col) & (row > 1), table[line + k], table[line + near + k])

        @pl.when(row > 0)
        def _():
            for i in range(count):

                @pl.when(slot == i)
                def _():
                    at = jnp.where(row == 1, 0, col)
                    pltpu.make_async_copy(own[i], wg.at[k, at], sems.at[1, k]).start()
                    pltpu.make_async_copy(sib[i], wg.at[k, 1 - at], sems.at[2, k]).start()

        return 0

    lax.fori_loop(0, owned, start, 0)
    wait(inv, sem.at[0])
    wait(w01, sem.at[1])
    wait(wr.at[0], sem.at[2])
    wait(wr.at[1], sem.at[3])

    def end(k, _):
        wait(tiles.at[k], sems.at[0, k])

        @pl.when(row > 0)
        def _():
            wait(wg.at[k, 0], sems.at[1, k])
            wait(wg.at[k, 1], sems.at[2, k])

        return 0

    lax.fori_loop(0, owned, end, 0)
    inverse = split(inv[...])
    cross = split(w01[...])

    @pl.when(odd == 0)
    def _():
        w01[...] = three(inverse, cross, 1, 0).T

    @pl.when(odd != 0)
    def _():
        w01[...] = three(cross, inverse, 1, 1)

    p01 = split(w01[...])
    solved = three(split(wr[0]), inverse, 1, 1)
    p0[...] = jnp.where(row == 0, lower_part(solved), solved)
    mine = split(p0[...])
    t1r[...] = wr[1] - three(mine, p01, 1, 1)

    def body(k, _):
        @pl.when(row > 1)
        def _():
            g = three(split(wg[k, 0]), inverse, 1, 1)
            parts = split(g)
            t1g[k] = wg[k, 1] - three(parts, p01, 1, 1)
            acc[k] = tiles[k] - three(mine, parts, 1, 1)

        @pl.when(row == 1)
        def _():
            g = split(three(inverse, split(wg[k, 0]), 1, 0))
            t1g[k] = (tiles[k] - three(p01, g, 1, 0)).T
            acc[k] = tiles[k] - three(mine, g, 1, 0)

        @pl.when(row == 0)
        def _():
            g = split(three(inverse, split(tiles[k]), 1, 0))
            t1g[k] = jnp.zeros_like(tiles[k])
            acc[k] = tiles[k] - three(mine, g, 1, 0)

        return 0

    lax.fori_loop(0, owned, body, 0, unroll=2)


def late_kernel(owned, col_total, p0, t1r, t1g, acc, inv_own, inv_sib, out, inv, p1, res, sem, sems):
    row, col, layer = place()

    @pl.when(col == 0)
    def _():
        pltpu.make_async_copy(inv_own, inv, sem.at[0]).start()

    @pl.when(col != 0)
    def _():
        pltpu.make_async_copy(inv_sib, inv, sem.at[0]).start()

    pltpu.make_async_copy(inv_own, inv, sem.at[0]).wait()
    inverse = split(inv[...])
    solved = three(split(t1r[...]), inverse, 1, 1)
    solved = jnp.where(row == 1, lower_part(solved), solved)
    p1[...] = jnp.where(row == 0, 0.0, solved)
    mine = split(p1[...])

    def out_copy(k):
        return pltpu.make_async_copy(
            res.at[k], out.at[0, 0, :, k, 0, :], sems.at[k]
        )

    def body(k, _):
        block = (layer * owned + k) * col_total + col

        @pl.when(block == 0)
        def _():
            res[k] = p0[...]

        @pl.when(block == 1)
        def _():
            res[k] = p1[...]

        @pl.when(block > 1)
        def _():
            g = three(split(t1g[k]), inverse, 1, 1)
            res[k] = acc[k] - three(mine, split(g), 1, 1)

        out_copy(k).start()
        return 0

    lax.fori_loop(0, owned, body, 0, unroll=2)

    def end(k, _):
        out_copy(k).wait()
        return 0

    lax.fori_loop(0, owned, end, 0)


def call_early(dims, table, matrix, own, sib, inv_own, inv_sib):
    owned = dims[1]
    n = matrix.shape[2]
    block = jax.ShapeDtypeStruct((n, n), F32)
    stack = jax.ShapeDtypeStruct((owned, n, n), F32)
    dma = pltpu.SemaphoreType.DMA
    return pl.pallas_call(
        functools.partial(early_kernel, dims),
        out_shape=(block, block, stack, stack),
        in_specs=[SMEM] + [ANY] * (2 * len(own) + 3),
        out_specs=(VMEM,) * 4,
        scratch_shapes=[
            pltpu.VMEM((n, n), F32),
            pltpu.VMEM((n, n), F32),
            pltpu.VMEM((2, n, n), F32),
            pltpu.VMEM((owned, 2, n, n), F32),
            pltpu.VMEM((owned, n, n), F32),
            dma((4,)),
            dma((3, owned)),
        ],
        cost_estimate=pl.CostEstimate(flops=60 * n**3, transcendentals=0, bytes_accessed=32 * n * n * 4),
        name="early",
    )(table, matrix, *own, *sib, inv_own, inv_sib)


def call_late(col_total, p0, t1r, t1g, acc, inv_own, inv_sib):
    owned, n, _ = acc.shape
    dma = pltpu.SemaphoreType.DMA
    return pl.pallas_call(
        functools.partial(late_kernel, owned, col_total),
        out_shape=jax.ShapeDtypeStruct((1, 1, n, owned, 1, n), F32),
        in_specs=[VMEM] * 4 + [ANY] * 2,
        out_specs=ANY,
        scratch_shapes=[
            pltpu.VMEM((n, n), F32),
            pltpu.VMEM((n, n), F32),
            pltpu.VMEM((owned, n, n), F32),
            dma((1,)),
            dma((owned,)),
        ],
        cost_estimate=pl.CostEstimate(flops=30 * n**3, transcendentals=0, bytes_accessed=16 * n * n * 4),
        name="late",
    )(p0, t1r, t1g, acc, inv_own, inv_sib)


def put(rounds, pairs):
    for i, taken in enumerate(rounds):
        if all(s != a and t != b for s, t in pairs for a, b in taken):
            taken.extend(pairs)
            return i
    rounds.append(list(pairs))
    return len(rounds) - 1


def gather_plan(levels, near, layer_total, col_total):
    cores = range(col_total)
    rounds = [[((1, 1, l), (0, 0, l)) for l in range(layer_total)]]
    arrived = {}
    for l in range(layer_total):
        for gap in range(1, levels):
            for h in range(max(1, l * near), (l + 1) * near):
                for t in (h + gap, h - gap):
                    if 1 <= t < levels:
                        pairs = [
                            ((2 * h + y, c, l), (2 * t + y, c, l)) for y in range(2) for c in cores
                        ]
                        arrived[l, t, h] = put(rounds, pairs)
    for t in range(levels - 1, 0, -1):
        for l in range(layer_total):
            pairs = [((y, 1 - y, l), (2 * t + y, 1 - y, l)) for y in range(2)]
            arrived[l, t, "cross"] = put(rounds, pairs)
    return rounds, arrived


def pair_plan(levels, near, layer_total, count, arrived):
    plan = {}
    for l in range(layer_total):
        for t in range(levels):
            line = []
            for h in range(l * near, (l + 1) * near):
                if t == h and h > 0:
                    line.append((0, 0, h))
                elif (l, t, h) in arrived:
                    line.append((1, 1 + arrived[l, t, h], h))
            line.sort()
            step = {}
            for order, slot, h in line:
                j = max(0, slot - 1 - (count - near)) if order else 0
                while j in step:
                    j += 1
                step[j % near if j >= near else j] = (slot, h)
            plan[l, t] = step
    return plan


def on_device(matrix):
    row_total = lax.axis_size("row")
    col_total = lax.axis_size("col")
    layer_total = lax.axis_size("layer")
    row, col, layer = place()
    n = matrix.shape[2]
    col_blocks = matrix.shape[3]
    owned = col_blocks // layer_total
    levels = row_total // 2
    near = levels // layer_total
    swap = [(0, 1), (1, 0)]
    level = row // 2

    def device(r, c, l):
        return (r * col_total + c) * layer_total + l

    def permute(x, pairs):
        return lax.ppermute(x, AXES, [(device(*s), device(*t)) for s, t in pairs])

    def permute_rows(x, pairs, cores):
        return permute(
            x,
            [((a, c, l), (b, c, l)) for a, b in pairs for c in cores for l in range(layer_total)],
        )

    def sibling(x):
        return lax.ppermute(x, "col", swap)

    rounds, arrived = gather_plan(levels, near, layer_total, col_total)
    plan = pair_plan(levels, near, layer_total, len(rounds), arrived)

    mine = matrix[0, 0, :, 0, 0, :]
    inv0 = call_first(matrix, n)
    other = sibling(mine)
    got = [permute(mine, pairs) for pairs in rounds]
    inv1 = call_second(inv0, other, got[0])

    first = [0]
    hop = permute_rows(inv0, [(0, 1)], first)
    flat = [permute_rows(hop, [(1, 2 * t + 1)], first) for t in range(levels - 1, 0, -1)]
    odd_rows = sum(flat[1:], flat[0])
    back = permute_rows(odd_rows, [(2 * t + 1, 2 * t) for t in range(1, levels)], first)
    inv0_own = jnp.where(row == 0, inv0, jnp.where(row == 1, hop, jnp.where(row % 2 == 1, odd_rows, back)))
    inv0_sib = sibling(inv0_own)

    flat = [permute_rows(inv1, [(0, 2 * t)], first) for t in range(levels - 1, 0, -1)]
    hop = permute_rows(inv1, [(0, 1)], first)
    even_rows = sum(flat[1:], flat[0])
    back = permute_rows(even_rows, [(2 * t, 2 * t + 1) for t in range(1, levels)], first)
    inv1_own = jnp.where(row == 0, inv1, jnp.where(row == 1, hop, jnp.where(row % 2 == 1, back, even_rows)))
    inv1_sib = sibling(inv1_own)

    own = [mine] + got
    for j in range(near):
        send = lax.dynamic_index_in_dim(matrix, layer * owned + j, 3, keepdims=False)[0, 0, :, 0, :]
        pairs = [((0, c, l), (1, c, l)) for c in range(col_total) for l in range(layer_total)]
        users = {}
        for (l, t), step in plan.items():
            if j in step:
                users.setdefault(step[j][0], []).append((l, t))
                for c in range(col_total):
                    pairs += [((2 * t + y, c, l), (2 * t + 1 - y, c, l)) for y in range(2)]
        for slot, who in users.items():
            chosen = functools.reduce(
                jnp.logical_or, [(layer == l) & (level == t) for l, t in who]
            )
            send = jnp.where(chosen, own[slot], send)
        own.append(permute(send, pairs))
    sib = [other] + [sibling(x) for x in own[1:]]

    table = []
    for l in range(layer_total):
        for t in range(levels):
            slots = {h: (slot, 1 + len(rounds) + j) for j, (slot, h) in plan[l, t].items()}
            near_rows = range(l * near, (l + 1) * near)
            table += [slots.get(h, (0, 0))[0] for h in near_rows]
            if t:
                table += [slots.get(h, (0, 0))[1] for h in near_rows]
            else:
                table += [1 + len(rounds) + j for j in range(near)]
            table.append(1 + arrived[l, t, "cross"] if t else 0)
    dims = (len(own), owned, near, levels)
    p0, t1r, t1g, acc = call_early(
        dims, jnp.array(table, jnp.int32), matrix, own, sib, inv0_own, inv0_sib
    )
    return call_late(col_total, p0, t1r, t1g, acc, inv1_own, inv1_sib)


def solution(mesh):
    in_specs = (P(None, "row", None, None, "col", None),)
    out_specs = P(None, "row", None, "layer", "col", None)
    return jax.shard_map(
        on_device, mesh=mesh, in_specs=in_specs, out_specs=out_specs, check_vma=False
    )
```

```python
import functools

import jax
import jax.numpy as jnp
from jax import lax
from jax.experimental import pallas as pl
from jax.experimental.pallas import tpu as pltpu
from jax.sharding import PartitionSpec as P


HIGH = lax.Precision.HIGHEST
F32 = jnp.float32
AXES = ("row", "col", "layer")
VMEM = pl.BlockSpec(memory_space=pltpu.VMEM)
SMEM = pl.BlockSpec(memory_space=pltpu.SMEM)
ANY = pl.BlockSpec(memory_space=pl.ANY)
HBM = pl.BlockSpec(memory_space=pltpu.HBM)
LANES = 128
SUB = 8


def contract(left, right, ldim, rdim):
    return lax.dot_general(
        left,
        right,
        (((ldim,), (rdim,)), ((), ())),
        precision=HIGH,
        preferred_element_type=F32,
    )


def nn(a, b):
    return contract(a, b, 1, 0)


def tn(a, b):
    return contract(a, b, 0, 0)


def row_of(tile, k):
    return jnp.broadcast_to(tile[k : k + 1, :], tile.shape)


def small_inverse(block):
    size = block.shape[0]
    tiles = size // SUB
    width = 2 * size
    rows = lax.broadcasted_iota(jnp.int32, (size, size), 0)
    cols = lax.broadcasted_iota(jnp.int32, (size, size), 1)
    eye = jnp.where(rows == cols, 1.0, 0.0).astype(F32)
    full = jnp.concatenate([block, eye], axis=1)
    v = [full[SUB * t : SUB * (t + 1)] for t in range(tiles)]
    sub = lax.broadcasted_iota(jnp.int32, (SUB, width), 0)
    for s in range(tiles):
        c = {
            (j, t): jnp.broadcast_to(v[t][:, SUB * s + j : SUB * s + j + 1], (SUB, width))
            for j in range(SUB)
            for t in range(s, tiles)
        }
        pivots = jnp.ones((SUB, width), F32)
        for k in range(0, SUB, 2):
            p = row_of(c[k, s], k)
            q = row_of(c[k, s], k + 1)
            w = row_of(c[k + 1, s], k + 1)
            det = p * w - q * q
            over_det = 1.0 / det
            over_p = 1.0 / p
            v0, v1 = row_of(v[s], k), row_of(v[s], k + 1)
            c0 = {j: row_of(c[j, s], k) for j in range(k + 2, SUB)}
            c1 = {j: row_of(c[j, s], k + 1) for j in range(k + 2, SUB)}
            pivots = jnp.where(sub == k, p, jnp.where(sub == k + 1, det * over_p, pivots))
            for t in range(s, tiles):
                m0 = (w * c[k, t] - q * c[k + 1, t]) * over_det
                m1 = (p * c[k + 1, t] - q * c[k, t]) * over_det
                if t == s:
                    m0 = jnp.where(sub > k + 1, m0, jnp.where(sub == k + 1, q * over_p, 0.0))
                    m1 = jnp.where(sub > k + 1, m1, 0.0)
                v[t] = v[t] - m0 * v0 - m1 * v1
                for j in range(k + 2, SUB):
                    c[j, t] = c[j, t] - m0 * c0[j] - m1 * c1[j]
        v[s] = v[s] * lax.rsqrt(pivots)
    return jnp.concatenate(v, axis=0)[:, size:]


def inverse_factor(a, x):
    n = a.shape[0]
    base = min(n, LANES // 2)
    x[...] = jnp.zeros((n, n), F32)
    for lo in range(0, n, base):
        hi = lo + base
        inv = small_inverse(a[lo:hi, lo:hi])
        if lo:
            x[lo:hi, :lo] = nn(inv, x[lo:hi, :lo])
        x[lo:hi, lo:hi] = inv
        if hi < n:
            upper = nn(inv, a[lo:hi, hi:])
            a[hi:, hi:] = a[hi:, hi:] - tn(upper, upper)
            x[hi:, :hi] = x[hi:, :hi] - tn(upper, x[lo:hi, :hi])


def split(x):
    high = x.astype(jnp.bfloat16)
    return high, (x - high.astype(F32)).astype(jnp.bfloat16)


def three(left, right, ldim, rdim):
    def part(a, b):
        return lax.dot_general(
            a, b, (((ldim,), (rdim,)), ((), ())), preferred_element_type=F32
        )

    return part(left[0], right[0]) + (part(left[0], right[1]) + part(left[1], right[0]))


def lower_part(x):
    rows = lax.broadcasted_iota(jnp.int32, x.shape, 0)
    cols = lax.broadcasted_iota(jnp.int32, x.shape, 1)
    return jnp.where(rows >= cols, x, 0.0)


def place():
    return lax.axis_index("row"), lax.axis_index("col"), lax.axis_index("layer")


def is_owner():
    row, col, _ = place()
    return (row == 0) & (col == 0)


def first_kernel(w00, inv, a):
    @pl.when(is_owner())
    def _():
        a[...] = w00[...]
        inverse_factor(a, inv)

    @pl.when(jnp.logical_not(is_owner()))
    def _():
        inv[...] = jnp.zeros_like(inv)


def second_kernel(inv0, w01, w11, matrix, inv1, tiles, a, sems):
    row, _, layer = place()
    owned = tiles.shape[0]

    def tile_copy(k):
        return pltpu.make_async_copy(
            matrix.at[0, 0, :, layer * owned + k, 0, :], tiles.at[k], sems.at[k]
        )

    @pl.when(row == 0)
    def _():
        for k in range(owned):
            tile_copy(k).start()

    @pl.when(is_owner())
    def _():
        q = nn(inv0[...], w01[...])
        a[...] = w11[...] - tn(q, q)
        inverse_factor(a, inv1)

    @pl.when(jnp.logical_not(is_owner()))
    def _():
        inv1[...] = jnp.zeros_like(inv1)

    @pl.when(row == 0)
    def _():
        for k in range(owned):
            tile_copy(k).wait()


def lookup(slots):
    row, _, layer = place()
    value = jnp.int32(0)
    for (l, t), slot in slots.items():
        value = jnp.where((layer == l) & (row // 2 == t), slot, value)
    return value


def pick_kernel(slots, *refs):
    *sources, out = refs
    slot = lookup(slots)
    for i, source in enumerate(sources):

        @pl.when(slot == i)
        def _():
            out[...] = source[...]


def grant(n, blocks):
    return pltpu.CompilerParams(vmem_limit_bytes=(blocks + 12) * n * n * 4)


def factor_cost(n):
    return pl.CostEstimate(flops=40 * n**3, transcendentals=0, bytes_accessed=64 * n * n * 4)


def call_first(w00):
    n = w00.shape[0]
    return pl.pallas_call(
        first_kernel,
        out_shape=jax.ShapeDtypeStruct((n, n), F32),
        in_specs=[VMEM],
        out_specs=VMEM,
        scratch_shapes=[pltpu.VMEM((n, n), F32)],
        cost_estimate=factor_cost(n),
        compiler_params=grant(n, 3),
        name="first",
    )(w00)


def call_second(inv0, w01, w11, matrix, owned):
    n = w11.shape[0]
    return pl.pallas_call(
        second_kernel,
        out_shape=(
            jax.ShapeDtypeStruct((n, n), F32),
            jax.ShapeDtypeStruct((owned, n, n), F32),
        ),
        in_specs=[VMEM] * 3 + [HBM],
        out_specs=(VMEM, VMEM),
        scratch_shapes=[pltpu.VMEM((n, n), F32), pltpu.SemaphoreType.DMA((owned,))],
        cost_estimate=factor_cost(n),
        compiler_params=grant(n, 5 + owned),
        name="second",
    )(inv0, w01, w11, matrix)


def call_pick(slots, sources):
    n = sources[0].shape[0]
    return pl.pallas_call(
        functools.partial(pick_kernel, slots),
        out_shape=jax.ShapeDtypeStruct((n, n), F32),
        in_specs=[VMEM] * len(sources),
        out_specs=VMEM,
        compiler_params=grant(n, 1 + len(sources)),
        name="pick",
    )(*sources)


def early_kernel(dims, table, matrix, above, *refs):
    count, owned, near, levels = dims
    own, sib = refs[:count], refs[count : 2 * count]
    inv_own, inv_sib = refs[2 * count : 2 * count + 2]
    p0, t1r, t1g, acc = refs[2 * count + 2 : 2 * count + 6]
    inv, w01, wr, wg, sems = refs[2 * count + 6 :]
    row, col, layer = place()
    level, odd = row // 2, row % 2

    def tile_copy(k):
        return pltpu.make_async_copy(
            matrix.at[0, 0, :, layer * owned + k, 0, :], acc.at[k], sems.at[k]
        )

    for k in range(owned):
        tile_copy(k).start()

    @pl.when(col == 1)
    def _():
        inv[...] = inv_own[...]

    @pl.when(col != 1)
    def _():
        inv[...] = inv_sib[...]

    line = (layer * levels + level) * (2 * near + 1)
    slot = table[line + 2 * near]
    for i in range(count):

        @pl.when((slot == i) & (col != odd))
        def _():
            w01[...] = own[i][...]

        @pl.when((slot == i) & (col == odd))
        def _():
            w01[...] = sib[i][...]

    wr[col] = own[0][...]
    wr[1 - col] = sib[0][...]

    def gather(k, _):
        slot = jnp.where(odd == col, table[line + k], table[line + near + k])
        for i in range(count):

            @pl.when((slot == i) & (row > 1))
            def _():
                wg[k, col] = own[i][...]
                wg[k, 1 - col] = sib[i][...]

        return 0

    lax.fori_loop(0, owned, gather, 0)
    inverse = split(inv[...])
    cross = split(w01[...])

    @pl.when(odd == 0)
    def _():
        w01[...] = three(inverse, cross, 1, 0).T

    @pl.when(odd != 0)
    def _():
        w01[...] = three(cross, inverse, 1, 1)

    p01 = split(w01[...])
    solved = three(split(wr[0]), inverse, 1, 1)
    p0[...] = jnp.where(row == 0, lower_part(solved), solved)
    mine = split(p0[...])
    t1r[...] = wr[1] - three(mine, p01, 1, 1)
    for k in range(owned):
        tile_copy(k).wait()

    def body(k, _):
        @pl.when(row > 1)
        def _():
            g = three(split(wg[k, 0]), inverse, 1, 1)
            parts = split(g)
            t1g[k] = wg[k, 1] - three(parts, p01, 1, 1)
            acc[k] = acc[k] - three(mine, parts, 1, 1)

        @pl.when(row == 1)
        def _():
            g = split(three(inverse, split(above[k]), 1, 0))
            t1g[k] = (acc[k] - three(p01, g, 1, 0)).T
            acc[k] = acc[k] - three(mine, g, 1, 0)

        @pl.when(row == 0)
        def _():
            g = split(three(inverse, split(acc[k]), 1, 0))
            t1g[k] = jnp.zeros_like(acc[k])
            acc[k] = acc[k] - three(mine, g, 1, 0)

        return 0

    lax.fori_loop(0, owned, body, 0, unroll=2)


def late_kernel(owned, col_total, p0, t1r, t1g, acc, inv_own, inv_sib, out, inv, p1, res, sems):
    row, col, layer = place()

    @pl.when(col == 0)
    def _():
        inv[...] = inv_own[...]

    @pl.when(col != 0)
    def _():
        inv[...] = inv_sib[...]

    inverse = split(inv[...])
    solved = three(split(t1r[...]), inverse, 1, 1)
    solved = jnp.where(row == 1, lower_part(solved), solved)
    p1[...] = jnp.where(row == 0, 0.0, solved)
    mine = split(p1[...])

    def out_copy(k):
        return pltpu.make_async_copy(
            res.at[k], out.at[0, 0, :, k, 0, :], sems.at[k]
        )

    def body(k, _):
        block = (layer * owned + k) * col_total + col

        @pl.when(block == 0)
        def _():
            res[k] = p0[...]

        @pl.when(block == 1)
        def _():
            res[k] = p1[...]

        @pl.when(block > 1)
        def _():
            g = three(split(t1g[k]), inverse, 1, 1)
            res[k] = acc[k] - three(mine, split(g), 1, 1)

        out_copy(k).start()
        return 0

    lax.fori_loop(0, owned, body, 0, unroll=2)

    def end(k, _):
        out_copy(k).wait()
        return 0

    lax.fori_loop(0, owned, end, 0)


def call_early(dims, table, matrix, above, own, sib, inv_own, inv_sib):
    owned = dims[1]
    n = matrix.shape[2]
    block = jax.ShapeDtypeStruct((n, n), F32)
    stack = jax.ShapeDtypeStruct((owned, n, n), F32)
    return pl.pallas_call(
        functools.partial(early_kernel, dims),
        out_shape=(block, block, stack, stack),
        in_specs=[SMEM, HBM] + [VMEM] * (2 * len(own) + 3),
        out_specs=(VMEM,) * 4,
        scratch_shapes=[
            pltpu.VMEM((n, n), F32),
            pltpu.VMEM((n, n), F32),
            pltpu.VMEM((2, n, n), F32),
            pltpu.VMEM((owned, 2, n, n), F32),
            pltpu.SemaphoreType.DMA((owned,)),
        ],
        cost_estimate=pl.CostEstimate(flops=60 * n**3, transcendentals=0, bytes_accessed=32 * n * n * 4),
        compiler_params=grant(n, 2 * len(own) + 8 + 6 * owned),
        name="early",
    )(table, matrix, above, *own, *sib, inv_own, inv_sib)


def call_late(col_total, p0, t1r, t1g, acc, inv_own, inv_sib):
    owned, n, _ = acc.shape
    return pl.pallas_call(
        functools.partial(late_kernel, owned, col_total),
        out_shape=jax.ShapeDtypeStruct((1, 1, n, owned, 1, n), F32),
        in_specs=[VMEM] * 6,
        out_specs=ANY,
        scratch_shapes=[
            pltpu.VMEM((n, n), F32),
            pltpu.VMEM((n, n), F32),
            pltpu.VMEM((owned, n, n), F32),
            pltpu.SemaphoreType.DMA((owned,)),
        ],
        cost_estimate=pl.CostEstimate(flops=30 * n**3, transcendentals=0, bytes_accessed=16 * n * n * 4),
        compiler_params=grant(n, 6 + 3 * owned),
        name="late",
    )(p0, t1r, t1g, acc, inv_own, inv_sib)


def put(rounds, pairs, start):
    for i, taken in enumerate(rounds):
        if i >= start and all(s != a and t != b for s, t in pairs for a, b in taken):
            taken.extend(pairs)
            return i
    rounds.append(list(pairs))
    return len(rounds) - 1


def gather_plan(levels, near, layer_total, col_total):
    cores = range(col_total)
    rounds = [[((1, 1, l), (0, 0, l)) for l in range(layer_total)]]
    arrived = {}
    for l in range(layer_total):
        rounds[0] += [((y, 1 - y, l), (2 + y, 1 - y, l)) for y in range(2)]
        arrived[l, 1, "cross"] = 0
    for l in range(layer_total):
        for gap in range(1, levels):
            for h in range(max(1, l * near), (l + 1) * near):
                for t in (h - gap, h + gap):
                    if 1 <= t < levels:
                        pairs = [
                            ((2 * h + y, c, l), (2 * t + y, c, l)) for y in range(2) for c in cores
                        ]
                        arrived[l, t, h] = put(rounds, pairs, 1)
    for t in range(levels - 1, 1, -1):
        for l in range(layer_total):
            pairs = [((y, 1 - y, l), (2 * t + y, 1 - y, l)) for y in range(2)]
            arrived[l, t, "cross"] = put(rounds, pairs, 1)
    return rounds, arrived


def pair_plan(levels, near, layer_total, count, arrived):
    plan = {}
    for l in range(layer_total):
        for t in range(levels):
            line = []
            for h in range(l * near, (l + 1) * near):
                if t == h and h > 0:
                    line.append((0, 0, h))
                elif (l, t, h) in arrived:
                    line.append((1, 1 + arrived[l, t, h], h))
            line.sort()
            step = {}
            for order, slot, h in line:
                j = max(0, slot - 2 - (count - 1 - near)) if order else 0
                while j in step:
                    j += 1
                step[j % near if j >= near else j] = (slot, h)
            plan[l, t] = step
    return plan


def on_device(matrix):
    row_total = lax.axis_size("row")
    col_total = lax.axis_size("col")
    layer_total = lax.axis_size("layer")
    col_blocks = matrix.shape[3]
    owned = col_blocks // layer_total
    levels = row_total // 2
    near = levels // layer_total
    swap = [(0, 1), (1, 0)]

    def device(r, c, l):
        return (r * col_total + c) * layer_total + l

    def permute(x, pairs):
        return lax.ppermute(x, AXES, [(device(*s), device(*t)) for s, t in pairs])

    def permute_rows(x, pairs, cores):
        return permute(
            x,
            [((a, c, l), (b, c, l)) for a, b in pairs for c in cores for l in range(layer_total)],
        )

    def sibling(x):
        return lax.ppermute(x, "col", swap)

    rounds, arrived = gather_plan(levels, near, layer_total, col_total)
    plan = pair_plan(levels, near, layer_total, len(rounds), arrived)
    first = [0]

    mine = matrix[0, 0, :, 0, 0, :]
    own = [mine]
    for pairs in rounds:
        own.append(permute(mine, pairs))
    other = sibling(mine)
    inv0 = call_first(mine)
    inv0_sib = permute(inv0, [((0, 0, l), (0, 1, l)) for l in range(layer_total)])
    inv1, tiles = call_second(inv0, other, own[1], matrix, owned)
    above = permute(
        tiles,
        [((0, c, l), (1, c, l)) for c in range(col_total) for l in range(layer_total)],
    )

    sent = []
    for t in range(levels - 1, 0, -1):
        sent.append(permute_rows(inv1, [(0, 2 * t)], first))
    hop = permute_rows(inv1, [(0, 1)], first)

    for j in range(near):
        slots = {key: step[j][0] for key, step in plan.items() if j in step}
        used = sorted(set(slots.values()))
        pairs = []
        for l, t in slots:
            for c in range(col_total):
                pairs += [((2 * t + y, c, l), (2 * t + 1 - y, c, l)) for y in range(2)]
        send = call_pick(
            {key: used.index(slot) for key, slot in slots.items()},
            [own[slot] for slot in used],
        )
        own.append(permute(send, pairs))

    even = inv0_sib
    gap = levels // 2
    while gap:
        pairs = [
            ((2 * t, 1, l), (2 * t + 2 * gap, 1, l))
            for t in range(0, levels, 2 * gap)
            for l in range(layer_total)
        ]
        even = even + permute(even, pairs)
        gap //= 2
    back = permute_rows(even, [(2 * t, 2 * t + 1) for t in range(levels)], [1])
    inv0_own = even + back
    inv0_sib = sibling(inv0_own)
    sib = [other]
    for x in own[1:]:
        sib.append(sibling(x))

    even = sum(sent, inv1)
    back = permute_rows(even, [(2 * t, 2 * t + 1) for t in range(1, levels)], first)
    table = []
    for l in range(layer_total):
        for t in range(levels):
            slots = {h: (slot, 1 + len(rounds) + j) for j, (slot, h) in plan[l, t].items()}
            near_rows = range(l * near, (l + 1) * near)
            table += [slots.get(h, (0, 0))[0] for h in near_rows]
            table += [slots.get(h, (0, 0))[1] for h in near_rows]
            table.append(1 + arrived[l, t, "cross"] if t else 0)
    dims = (len(own), owned, near, levels)
    p0, t1r, t1g, acc = call_early(
        dims, jnp.array(table, jnp.int32), matrix, above, own, sib, inv0_own, inv0_sib
    )
    even, hop, p0 = lax.optimization_barrier((even, hop, p0))
    inv1_own = even + hop + back
    inv1_sib = sibling(inv1_own)
    return call_late(col_total, p0, t1r, t1g, acc, inv1_own, inv1_sib)


def solution(mesh):
    in_specs = (P(None, "row", None, None, "col", None),)
    out_specs = P(None, "row", None, "layer", "col", None)
    levels = mesh.shape["row"] // 2
    _, _ = gather_plan(levels, levels // mesh.shape["layer"], mesh.shape["layer"], mesh.shape["col"])

    return jax.shard_map(
        on_device, mesh=mesh, in_specs=in_specs, out_specs=out_specs, check_vma=False
    )
```

```python
import functools

import jax
import jax.numpy as jnp
from jax import lax
from jax.experimental import pallas as pl
from jax.experimental.pallas import tpu as pltpu
from jax.sharding import PartitionSpec as P


HIGH = lax.Precision.HIGHEST
F32 = jnp.float32
AXES = ("row", "col", "layer")
VMEM = pl.BlockSpec(memory_space=pltpu.VMEM)
SMEM = pl.BlockSpec(memory_space=pltpu.SMEM)
ANY = pl.BlockSpec(memory_space=pl.ANY)
HBM = pl.BlockSpec(memory_space=pltpu.HBM)
LANES = 128
SUB = 8


def contract(left, right, ldim, rdim):
    return lax.dot_general(
        left,
        right,
        (((ldim,), (rdim,)), ((), ())),
        precision=HIGH,
        preferred_element_type=F32,
    )


def nn(a, b):
    return contract(a, b, 1, 0)


def tn(a, b):
    return contract(a, b, 0, 0)


def row_of(tile, k):
    return jnp.broadcast_to(tile[k : k + 1, :], tile.shape)


def lane_of(tile, lane):
    index = jnp.full(tile.shape, lane, jnp.int32)
    return jnp.take_along_axis(tile, index, axis=1)


def small_inverse(block):
    size = block.shape[0]
    tiles = size // SUB
    width = 2 * size
    rows = lax.broadcasted_iota(jnp.int32, (size, size), 0)
    cols = lax.broadcasted_iota(jnp.int32, (size, size), 1)
    eye = jnp.where(rows == cols, 1.0, 0.0).astype(F32)
    full = jnp.concatenate([block, eye], axis=1)
    v = [full[SUB * t : SUB * (t + 1)] for t in range(tiles)]
    sub = lax.broadcasted_iota(jnp.int32, (SUB, width), 0)
    for s in range(tiles):
        c = {(j, t): lane_of(v[t], SUB * s + j) for j in range(SUB) for t in range(s, tiles)}
        pivots = jnp.ones((SUB, width), F32)
        for k in range(0, SUB, 2):
            p = row_of(c[k, s], k)
            q = row_of(c[k, s], k + 1)
            w = row_of(c[k + 1, s], k + 1)
            det = p * w - q * q
            over_det = 1.0 / det
            over_p = 1.0 / p
            v0, v1 = row_of(v[s], k), row_of(v[s], k + 1)
            c0 = {j: row_of(c[j, s], k) for j in range(k + 2, SUB)}
            c1 = {j: row_of(c[j, s], k + 1) for j in range(k + 2, SUB)}
            pivots = jnp.where(sub == k, p, jnp.where(sub == k + 1, det * over_p, pivots))
            for t in range(s, tiles):
                m0 = w * c[k, t] - q * c[k + 1, t]
                m1 = p * c[k + 1, t] - q * c[k, t]
                for j in range(k + 2, SUB):
                    c[j, t] = c[j, t] - (m0 * c0[j] + m1 * c1[j]) * over_det
                if t == s:
                    m0 = jnp.where(
                        sub > k + 1, m0 * over_det, jnp.where(sub == k + 1, q * over_p, 0.0)
                    )
                    m1 = jnp.where(sub > k + 1, m1 * over_det, 0.0)
                    v[t] = v[t] - (m0 * v0 + m1 * v1)
                else:
                    v[t] = v[t] - (m0 * v0 + m1 * v1) * over_det
        v[s] = v[s] * lax.rsqrt(pivots)
    return jnp.concatenate(v, axis=0)[:, size:]


def inverse_factor(a, x):
    n = a.shape[0]
    base = min(n, LANES // 2)
    x[...] = jnp.zeros((n, n), F32)
    diagonal = a[:base, :base]
    for lo in range(0, n, base):
        hi, end = lo + base, lo + 2 * base
        inv = small_inverse(diagonal)
        if hi < n:
            upper = nn(inv, a[lo:hi, hi:end])
            diagonal = a[hi:end, hi:end] - tn(upper, upper)
        if lo:
            x[lo:hi, :lo] = nn(inv, x[lo:hi, :lo])
        x[lo:hi, lo:hi] = inv
        if hi < n:
            x[hi:end, :hi] = x[hi:end, :hi] - tn(upper, x[lo:hi, :hi])
        if end < n:
            rest = nn(inv, a[lo:hi, end:])
            a[hi:end, end:] = a[hi:end, end:] - tn(upper, rest)
            a[end:, end:] = a[end:, end:] - tn(rest, rest)
            x[end:, :hi] = x[end:, :hi] - tn(rest, x[lo:hi, :hi])


def split(x):
    high = x.astype(jnp.bfloat16)
    return high, (x - high.astype(F32)).astype(jnp.bfloat16)


def three(left, right, ldim, rdim):
    def part(a, b):
        return lax.dot_general(
            a, b, (((ldim,), (rdim,)), ((), ())), preferred_element_type=F32
        )

    return part(left[0], right[0]) + (part(left[0], right[1]) + part(left[1], right[0]))


def lower_part(x):
    rows = lax.broadcasted_iota(jnp.int32, x.shape, 0)
    cols = lax.broadcasted_iota(jnp.int32, x.shape, 1)
    return jnp.where(rows >= cols, x, 0.0)


def place():
    return lax.axis_index("row"), lax.axis_index("col"), lax.axis_index("layer")


def is_owner():
    row, col, _ = place()
    return (row == 0) & (col == 0)


def first_kernel(w00, inv, a):
    @pl.when(is_owner())
    def _():
        a[...] = w00[...]
        inverse_factor(a, inv)

    @pl.when(jnp.logical_not(is_owner()))
    def _():
        inv[...] = jnp.zeros_like(inv)


def second_kernel(inv0, w01, w11, matrix, inv1, tiles, a, sems):
    row, _, layer = place()
    owned = tiles.shape[0]

    def tile_copy(k):
        return pltpu.make_async_copy(
            matrix.at[0, 0, :, layer * owned + k, 0, :], tiles.at[k], sems.at[k]
        )

    @pl.when(row == 0)
    def _():
        for k in range(owned):
            tile_copy(k).start()

    @pl.when(is_owner())
    def _():
        q = nn(inv0[...], w01[...])
        a[...] = w11[...] - tn(q, q)
        inverse_factor(a, inv1)

    @pl.when(jnp.logical_not(is_owner()))
    def _():
        inv1[...] = jnp.zeros_like(inv1)

    @pl.when(row == 0)
    def _():
        for k in range(owned):
            tile_copy(k).wait()


def lookup(slots):
    row, _, layer = place()
    value = jnp.int32(0)
    for (l, t), slot in slots.items():
        value = jnp.where((layer == l) & (row // 2 == t), slot, value)
    return value


def pick_kernel(slots, *refs):
    *sources, out = refs
    slot = lookup(slots)
    for i, source in enumerate(sources):

        @pl.when(slot == i)
        def _():
            out[...] = source[...]


def grant(n, blocks):
    return pltpu.CompilerParams(vmem_limit_bytes=(blocks + 12) * n * n * 4)


def factor_cost(n):
    return pl.CostEstimate(flops=40 * n**3, transcendentals=0, bytes_accessed=64 * n * n * 4)


def call_first(w00):
    n = w00.shape[0]
    return pl.pallas_call(
        first_kernel,
        out_shape=jax.ShapeDtypeStruct((n, n), F32),
        in_specs=[VMEM],
        out_specs=VMEM,
        scratch_shapes=[pltpu.VMEM((n, n), F32)],
        cost_estimate=factor_cost(n),
        compiler_params=grant(n, 3),
        name="first",
    )(w00)


def call_second(inv0, w01, w11, matrix, owned):
    n = w11.shape[0]
    return pl.pallas_call(
        second_kernel,
        out_shape=(
            jax.ShapeDtypeStruct((n, n), F32),
            jax.ShapeDtypeStruct((owned, n, n), F32),
        ),
        in_specs=[VMEM] * 3 + [HBM],
        out_specs=(VMEM, VMEM),
        scratch_shapes=[pltpu.VMEM((n, n), F32), pltpu.SemaphoreType.DMA((owned,))],
        cost_estimate=factor_cost(n),
        compiler_params=grant(n, 5 + owned),
        name="second",
    )(inv0, w01, w11, matrix)


def call_pick(slots, sources):
    n = sources[0].shape[0]
    return pl.pallas_call(
        functools.partial(pick_kernel, slots),
        out_shape=jax.ShapeDtypeStruct((n, n), F32),
        in_specs=[VMEM] * len(sources),
        out_specs=VMEM,
        compiler_params=grant(n, 1 + len(sources)),
        name="pick",
    )(*sources)


def early_kernel(dims, table, matrix, above, *refs):
    count, owned, near, levels = dims
    own, sib = refs[:count], refs[count : 2 * count]
    inv_own, inv_sib = refs[2 * count : 2 * count + 2]
    p0, t1r, t1g, acc = refs[2 * count + 2 : 2 * count + 6]
    inv, w01, wr, wg, sems = refs[2 * count + 6 :]
    row, col, layer = place()
    level, odd = row // 2, row % 2

    def tile_copy(k):
        return pltpu.make_async_copy(
            matrix.at[0, 0, :, layer * owned + k, 0, :], acc.at[k], sems.at[k]
        )

    for k in range(owned):
        tile_copy(k).start()

    @pl.when(col == 1)
    def _():
        inv[...] = inv_own[...]

    @pl.when(col != 1)
    def _():
        inv[...] = inv_sib[...]

    line = (layer * levels + level) * (2 * near + 1)
    slot = table[line + 2 * near]
    for i in range(count):

        @pl.when((slot == i) & (col != odd))
        def _():
            w01[...] = own[i][...]

        @pl.when((slot == i) & (col == odd))
        def _():
            w01[...] = sib[i][...]

    wr[col] = own[0][...]
    wr[1 - col] = sib[0][...]

    def gather(k, _):
        slot = jnp.where(odd == col, table[line + k], table[line + near + k])
        for i in range(count):

            @pl.when((slot == i) & (row > 1))
            def _():
                wg[k, col] = own[i][...]
                wg[k, 1 - col] = sib[i][...]

        return 0

    lax.fori_loop(0, owned, gather, 0)
    inverse = split(inv[...])
    cross = split(w01[...])

    @pl.when(odd == 0)
    def _():
        w01[...] = three(inverse, cross, 1, 0).T

    @pl.when(odd != 0)
    def _():
        w01[...] = three(cross, inverse, 1, 1)

    p01 = split(w01[...])
    solved = three(split(wr[0]), inverse, 1, 1)
    p0[...] = jnp.where(row == 0, lower_part(solved), solved)
    mine = split(p0[...])
    t1r[...] = wr[1] - three(mine, p01, 1, 1)
    for k in range(owned):
        tile_copy(k).wait()

    def body(k, _):
        @pl.when(row > 1)
        def _():
            g = three(split(wg[k, 0]), inverse, 1, 1)
            parts = split(g)
            t1g[k] = wg[k, 1] - three(parts, p01, 1, 1)
            acc[k] = acc[k] - three(mine, parts, 1, 1)

        @pl.when(row == 1)
        def _():
            g = split(three(inverse, split(above[k]), 1, 0))
            t1g[k] = (acc[k] - three(p01, g, 1, 0)).T
            acc[k] = acc[k] - three(mine, g, 1, 0)

        @pl.when(row == 0)
        def _():
            g = split(three(inverse, split(acc[k]), 1, 0))
            t1g[k] = jnp.zeros_like(acc[k])
            acc[k] = acc[k] - three(mine, g, 1, 0)

        return 0

    lax.fori_loop(0, owned, body, 0, unroll=2)


def late_kernel(owned, col_total, p0, t1r, t1g, acc, inv_own, inv_sib, out, inv, p1, res, sems):
    row, col, layer = place()

    @pl.when(col == 0)
    def _():
        inv[...] = inv_own[...]

    @pl.when(col != 0)
    def _():
        inv[...] = inv_sib[...]

    inverse = split(inv[...])
    solved = three(split(t1r[...]), inverse, 1, 1)
    solved = jnp.where(row == 1, lower_part(solved), solved)
    p1[...] = jnp.where(row == 0, 0.0, solved)
    mine = split(p1[...])

    def out_copy(k):
        return pltpu.make_async_copy(
            res.at[k], out.at[0, 0, :, k, 0, :], sems.at[k]
        )

    def body(k, _):
        block = (layer * owned + k) * col_total + col

        @pl.when(block == 0)
        def _():
            res[k] = p0[...]

        @pl.when(block == 1)
        def _():
            res[k] = p1[...]

        @pl.when(block > 1)
        def _():
            g = three(split(t1g[k]), inverse, 1, 1)
            res[k] = acc[k] - three(mine, split(g), 1, 1)

        out_copy(k).start()
        return 0

    lax.fori_loop(0, owned, body, 0, unroll=2)

    def end(k, _):
        out_copy(k).wait()
        return 0

    lax.fori_loop(0, owned, end, 0)


def call_early(dims, table, matrix, above, own, sib, inv_own, inv_sib):
    owned = dims[1]
    n = matrix.shape[2]
    block = jax.ShapeDtypeStruct((n, n), F32)
    stack = jax.ShapeDtypeStruct((owned, n, n), F32)
    return pl.pallas_call(
        functools.partial(early_kernel, dims),
        out_shape=(block, block, stack, stack),
        in_specs=[SMEM, HBM] + [VMEM] * (2 * len(own) + 3),
        out_specs=(VMEM,) * 4,
        scratch_shapes=[
            pltpu.VMEM((n, n), F32),
            pltpu.VMEM((n, n), F32),
            pltpu.VMEM((2, n, n), F32),
            pltpu.VMEM((owned, 2, n, n), F32),
            pltpu.SemaphoreType.DMA((owned,)),
        ],
        cost_estimate=pl.CostEstimate(flops=60 * n**3, transcendentals=0, bytes_accessed=32 * n * n * 4),
        compiler_params=grant(n, 2 * len(own) + 8 + 6 * owned),
        name="early",
    )(table, matrix, above, *own, *sib, inv_own, inv_sib)


def call_late(col_total, p0, t1r, t1g, acc, inv_own, inv_sib):
    owned, n, _ = acc.shape
    return pl.pallas_call(
        functools.partial(late_kernel, owned, col_total),
        out_shape=jax.ShapeDtypeStruct((1, 1, n, owned, 1, n), F32),
        in_specs=[VMEM] * 6,
        out_specs=ANY,
        scratch_shapes=[
            pltpu.VMEM((n, n), F32),
            pltpu.VMEM((n, n), F32),
            pltpu.VMEM((owned, n, n), F32),
            pltpu.SemaphoreType.DMA((owned,)),
        ],
        cost_estimate=pl.CostEstimate(flops=30 * n**3, transcendentals=0, bytes_accessed=16 * n * n * 4),
        compiler_params=grant(n, 6 + 3 * owned),
        name="late",
    )(p0, t1r, t1g, acc, inv_own, inv_sib)


def put(rounds, choices):
    for i, taken in enumerate(rounds):
        for k in range(len(choices)):
            pairs = choices[(i - 1 + k) % len(choices)]
            if i and all(s != a and t != b for s, t in pairs for a, b in taken):
                taken.extend(pairs)
                return i
    rounds.append(list(choices[(len(rounds) - 1) % len(choices)]))
    return len(rounds) - 1


def gather_plan(levels, near, layer_total, col_total):
    cores = range(col_total)
    rounds = [[((1, 1, l), (0, 0, l)) for l in range(layer_total)]]
    arrived = {}
    for l in range(layer_total):
        rounds[0] += [((y, 1 - y, l), (2 + y, 1 - y, l)) for y in range(2)]
        arrived[l, 1, "cross"] = 0
    for t in range(levels - 1, 1, -1):
        for l in range(layer_total):
            pairs = [((y, 1 - y, l), (2 * t + y, 1 - y, l)) for y in range(2)]
            arrived[l, t, "cross"] = put(rounds, [pairs])
    for l in range(layer_total):
        for gap in range(1, levels):
            for h in range(max(1, l * near), (l + 1) * near):
                for t in (h - gap, h + gap):
                    if 1 <= t < levels:
                        arrived[l, t, h] = put(
                            rounds,
                            [
                                [
                                    ((2 * h + y, c, (l + k) % layer_total), (2 * t + y, c, l))
                                    for y in range(2)
                                    for c in cores
                                ]
                                for k in range(layer_total)
                            ],
                        )
    return rounds, arrived


def pair_plan(levels, near, layer_total, count, arrived):
    plan = {}
    for l in range(layer_total):
        for t in range(levels):
            line = []
            for h in range(l * near, (l + 1) * near):
                if t == h and h > 0:
                    line.append((0, 0, h))
                elif (l, t, h) in arrived:
                    line.append((1, 1 + arrived[l, t, h], h))
            line.sort()
            step = {}
            for order, slot, h in line:
                j = max(0, slot - 2 - (count - 1 - near)) if order else 0
                while j in step:
                    j += 1
                step[j % near if j >= near else j] = (slot, h)
            plan[l, t] = step
    return plan


def on_device(matrix):
    row_total = lax.axis_size("row")
    col_total = lax.axis_size("col")
    layer_total = lax.axis_size("layer")
    col_blocks = matrix.shape[3]
    owned = col_blocks // layer_total
    levels = row_total // 2
    near = levels // layer_total
    swap = [(0, 1), (1, 0)]

    def device(r, c, l):
        return (r * col_total + c) * layer_total + l

    def permute(x, pairs):
        return lax.ppermute(x, AXES, [(device(*s), device(*t)) for s, t in pairs])

    def permute_rows(x, pairs, cores):
        return permute(
            x,
            [((a, c, l), (b, c, l)) for a, b in pairs for c in cores for l in range(layer_total)],
        )

    def sibling(x):
        return lax.ppermute(x, "col", swap)

    rounds, arrived = gather_plan(levels, near, layer_total, col_total)
    plan = pair_plan(levels, near, layer_total, len(rounds), arrived)
    first = [0]

    mine = matrix[0, 0, :, 0, 0, :]
    own = [mine]
    for pairs in rounds:
        own.append(permute(mine, pairs))
    other = sibling(mine)
    inv0 = call_first(mine)
    inv0_sib = permute(inv0, [((0, 0, l), (0, 1, l)) for l in range(layer_total)])
    inv1, tiles = call_second(inv0, other, own[1], matrix, owned)
    above = permute(
        tiles,
        [((0, c, l), (1, c, l)) for c in range(col_total) for l in range(layer_total)],
    )

    sent = []
    for t in range(levels - 1, 0, -1):
        sent.append(permute_rows(inv1, [(0, 2 * t)], first))
    hop = permute_rows(inv1, [(0, 1)], first)

    for j in range(near):
        slots = {key: step[j][0] for key, step in plan.items() if j in step}
        used = sorted(set(slots.values()))
        pairs = []
        for l, t in slots:
            for c in range(col_total):
                pairs += [((2 * t + y, c, l), (2 * t + 1 - y, c, l)) for y in range(2)]
        send = call_pick(
            {key: used.index(slot) for key, slot in slots.items()},
            [own[slot] for slot in used],
        )
        own.append(permute(send, pairs))

    spread = []
    for t in range(levels - 1, 0, -1):
        spread.append(permute(inv0_sib, [((0, 1, l), (2 * t, 1, l)) for l in range(layer_total)]))
    even = sum(spread, inv0_sib)
    back = permute_rows(even, [(2 * t, 2 * t + 1) for t in range(levels)], [1])
    inv0_own = even + back
    inv0_sib = sibling(inv0_own)
    sib = [other]
    for x in own[1:]:
        sib.append(sibling(x))

    even = sum(sent, inv1)
    back = permute_rows(even, [(2 * t, 2 * t + 1) for t in range(1, levels)], first)
    table = []
    for l in range(layer_total):
        for t in range(levels):
            slots = {h: (slot, 1 + len(rounds) + j) for j, (slot, h) in plan[l, t].items()}
            near_rows = range(l * near, (l + 1) * near)
            table += [slots.get(h, (0, 0))[0] for h in near_rows]
            table += [slots.get(h, (0, 0))[1] for h in near_rows]
            table.append(1 + arrived[l, t, "cross"] if t else 0)
    dims = (len(own), owned, near, levels)
    p0, t1r, t1g, acc = call_early(
        dims, jnp.array(table, jnp.int32), matrix, above, own, sib, inv0_own, inv0_sib
    )
    even, hop, p0 = lax.optimization_barrier((even, hop, p0))
    inv1_own = even + hop + back
    inv1_sib = sibling(inv1_own)
    return call_late(col_total, p0, t1r, t1g, acc, inv1_own, inv1_sib)


def solution(mesh):
    in_specs = (P(None, "row", None, None, "col", None),)
    out_specs = P(None, "row", None, "layer", "col", None)
    levels = mesh.shape["row"] // 2
    near = levels // mesh.shape["layer"]
    _, _ = gather_plan(levels, near, mesh.shape["layer"], mesh.shape["col"])

    return jax.shard_map(
        on_device, mesh=mesh, in_specs=in_specs, out_specs=out_specs, check_vma=False
    )
```

```python
import functools

import jax
import jax.numpy as jnp
from jax import lax
from jax.experimental import pallas as pl
from jax.experimental.pallas import tpu as pltpu
from jax.sharding import PartitionSpec as P


HIGH = lax.Precision.HIGHEST
F32 = jnp.float32
AXES = ("row", "col", "layer")
VMEM = pl.BlockSpec(memory_space=pltpu.VMEM)
SMEM = pl.BlockSpec(memory_space=pltpu.SMEM)
ANY = pl.BlockSpec(memory_space=pl.ANY)
HBM = pl.BlockSpec(memory_space=pltpu.HBM)
LANES = 128
SUB = 8


def contract(left, right, ldim, rdim):
    return lax.dot_general(
        left,
        right,
        (((ldim,), (rdim,)), ((), ())),
        precision=HIGH,
        preferred_element_type=F32,
    )


def nn(a, b):
    return contract(a, b, 1, 0)


def tn(a, b):
    return contract(a, b, 0, 0)


def row_of(tile, k):
    return jnp.broadcast_to(tile[k : k + 1, :], tile.shape)


def lane_of(tile, lane):
    index = jnp.full(tile.shape, lane, jnp.int32)
    return jnp.take_along_axis(tile, index, axis=1)


def small_inverse(block):
    size = block.shape[0]
    tiles = size // SUB
    width = 2 * size
    rows = lax.broadcasted_iota(jnp.int32, (size, size), 0)
    cols = lax.broadcasted_iota(jnp.int32, (size, size), 1)
    eye = jnp.where(rows == cols, 1.0, 0.0).astype(F32)
    full = jnp.concatenate([block, eye], axis=1)
    v = [full[SUB * t : SUB * (t + 1)] for t in range(tiles)]
    sub = lax.broadcasted_iota(jnp.int32, (SUB, width), 0)
    for s in range(tiles):
        c = {(j, t): lane_of(v[t], SUB * s + j) for j in range(SUB) for t in range(s, tiles)}
        pivots = jnp.ones((SUB, width), F32)
        for k in range(0, SUB, 2):
            p = row_of(c[k, s], k)
            q = row_of(c[k, s], k + 1)
            w = row_of(c[k + 1, s], k + 1)
            det = p * w - q * q
            over_det = 1.0 / det
            over_p = 1.0 / p
            v0, v1 = row_of(v[s], k), row_of(v[s], k + 1)
            c0 = {j: row_of(c[j, s], k) for j in range(k + 2, SUB)}
            c1 = {j: row_of(c[j, s], k + 1) for j in range(k + 2, SUB)}
            pivots = jnp.where(sub == k, p, jnp.where(sub == k + 1, det * over_p, pivots))
            for t in range(s, tiles):
                m0 = w * c[k, t] - q * c[k + 1, t]
                m1 = p * c[k + 1, t] - q * c[k, t]
                for j in range(k + 2, SUB):
                    c[j, t] = c[j, t] - (m0 * c0[j] + m1 * c1[j]) * over_det
                if t == s:
                    m0 = jnp.where(
                        sub > k + 1, m0 * over_det, jnp.where(sub == k + 1, q * over_p, 0.0)
                    )
                    m1 = jnp.where(sub > k + 1, m1 * over_det, 0.0)
                    v[t] = v[t] - (m0 * v0 + m1 * v1)
                else:
                    v[t] = v[t] - (m0 * v0 + m1 * v1) * over_det
        v[s] = v[s] * lax.rsqrt(pivots)
    return jnp.concatenate(v, axis=0)[:, size:]


def inverse_factor(a, x):
    n = a.shape[0]
    base = min(n, LANES // 2)
    x[...] = jnp.zeros((n, n), F32)
    diagonal = a[:base, :base]
    for lo in range(0, n, base):
        hi, end = lo + base, lo + 2 * base
        inv = small_inverse(diagonal)
        if hi < n:
            upper = nn(inv, a[lo:hi, hi:end])
            diagonal = a[hi:end, hi:end] - tn(upper, upper)
        if lo:
            x[lo:hi, :lo] = nn(inv, x[lo:hi, :lo])
        x[lo:hi, lo:hi] = inv
        if hi < n:
            x[hi:end, :hi] = x[hi:end, :hi] - tn(upper, x[lo:hi, :hi])
        if end < n:
            rest = nn(inv, a[lo:hi, end:])
            a[hi:end, end:] = a[hi:end, end:] - tn(upper, rest)
            a[end:, end:] = a[end:, end:] - tn(rest, rest)
            x[end:, :hi] = x[end:, :hi] - tn(rest, x[lo:hi, :hi])


def split(x):
    high = x.astype(jnp.bfloat16)
    return high, (x - high.astype(F32)).astype(jnp.bfloat16)


def three(left, right, ldim, rdim):
    def part(a, b):
        return lax.dot_general(
            a, b, (((ldim,), (rdim,)), ((), ())), preferred_element_type=F32
        )

    return part(left[0], right[0]) + (part(left[0], right[1]) + part(left[1], right[0]))


def lower_part(x):
    rows = lax.broadcasted_iota(jnp.int32, x.shape, 0)
    cols = lax.broadcasted_iota(jnp.int32, x.shape, 1)
    return jnp.where(rows >= cols, x, 0.0)


def place():
    return lax.axis_index("row"), lax.axis_index("col"), lax.axis_index("layer")


def is_owner():
    row, col, _ = place()
    return (row == 0) & (col == 0)


def pack(x, out):
    n = x.shape[0]
    half, quarter = n // 2, n // 4
    out[:half] = x[half:]
    out[half:, :half] = x[:quarter, :half]
    out[half:, half:] = x[quarter:half, :half]


def unpack(source, x):
    n = x.shape[0]
    half, quarter = n // 2, n // 4
    x[half:] = source[:half]
    x[:quarter, :half] = source[half:, :half]
    x[quarter:half, :half] = source[half:, half:]
    x[:half, half:] = jnp.zeros((half, half), F32)


def first_kernel(w00, inv, packed, a):
    @pl.when(is_owner())
    def _():
        a[...] = w00[...]
        inverse_factor(a, inv)
        pack(inv, packed)

    @pl.when(jnp.logical_not(is_owner()))
    def _():
        packed[...] = jnp.zeros_like(packed)


def second_kernel(inv0, w01, w11, matrix, packed, tiles, a, x, sems):
    row, _, layer = place()
    owned = tiles.shape[0]

    def tile_copy(k):
        return pltpu.make_async_copy(
            matrix.at[0, 0, :, layer * owned + k, 0, :], tiles.at[k], sems.at[k]
        )

    @pl.when(row == 0)
    def _():
        for k in range(owned):
            tile_copy(k).start()

    @pl.when(is_owner())
    def _():
        q = nn(inv0[...], w01[...])
        a[...] = w11[...] - tn(q, q)
        inverse_factor(a, x)
        pack(x, packed)

    @pl.when(jnp.logical_not(is_owner()))
    def _():
        packed[...] = jnp.zeros_like(packed)

    @pl.when(row == 0)
    def _():
        for k in range(owned):
            tile_copy(k).wait()


def lookup(slots):
    row, _, layer = place()
    value = jnp.int32(0)
    for (l, t), slot in slots.items():
        value = jnp.where((layer == l) & (row // 2 == t), slot, value)
    return value


def pick_kernel(slots, *refs):
    *sources, out = refs
    slot = lookup(slots)
    for i, source in enumerate(sources):

        @pl.when(slot == i)
        def _():
            out[...] = source[...]


def grant(n, blocks):
    return pltpu.CompilerParams(vmem_limit_bytes=(blocks + 12) * n * n * 4)


def factor_cost(n):
    return pl.CostEstimate(flops=40 * n**3, transcendentals=0, bytes_accessed=64 * n * n * 4)


def call_first(w00):
    n = w00.shape[0]
    return pl.pallas_call(
        first_kernel,
        out_shape=(
            jax.ShapeDtypeStruct((n, n), F32),
            jax.ShapeDtypeStruct((n - n // 4, n), F32),
        ),
        in_specs=[VMEM],
        out_specs=(VMEM, VMEM),
        scratch_shapes=[pltpu.VMEM((n, n), F32)],
        cost_estimate=factor_cost(n),
        compiler_params=grant(n, 4),
        name="first",
    )(w00)


def call_second(inv0, w01, w11, matrix, owned):
    n = w11.shape[0]
    return pl.pallas_call(
        second_kernel,
        out_shape=(
            jax.ShapeDtypeStruct((n - n // 4, n), F32),
            jax.ShapeDtypeStruct((owned, n, n), F32),
        ),
        in_specs=[VMEM] * 3 + [HBM],
        out_specs=(VMEM, VMEM),
        scratch_shapes=[pltpu.VMEM((n, n), F32)] * 2 + [pltpu.SemaphoreType.DMA((owned,))],
        cost_estimate=factor_cost(n),
        compiler_params=grant(n, 6 + owned),
        name="second",
    )(inv0, w01, w11, matrix)


def call_pick(slots, sources):
    n = sources[0].shape[0]
    return pl.pallas_call(
        functools.partial(pick_kernel, slots),
        out_shape=jax.ShapeDtypeStruct((n, n), F32),
        in_specs=[VMEM] * len(sources),
        out_specs=VMEM,
        compiler_params=grant(n, 1 + len(sources)),
        name="pick",
    )(*sources)


def early_kernel(dims, table, matrix, above, *refs):
    count, owned, near, levels = dims
    own, sib = refs[:count], refs[count : 2 * count]
    inv_own, inv_sib = refs[2 * count : 2 * count + 2]
    p0, t1r, t1g, acc = refs[2 * count + 2 : 2 * count + 6]
    inv, w01, wr, wg, sems = refs[2 * count + 6 :]
    row, col, layer = place()
    level, odd = row // 2, row % 2

    def tile_copy(k):
        return pltpu.make_async_copy(
            matrix.at[0, 0, :, layer * owned + k, 0, :], acc.at[k], sems.at[k]
        )

    for k in range(owned):
        tile_copy(k).start()

    @pl.when(col == 1)
    def _():
        unpack(inv_own, inv)

    @pl.when(col != 1)
    def _():
        unpack(inv_sib, inv)

    line = (layer * levels + level) * (2 * near + 1)
    slot = table[line + 2 * near]
    for i in range(count):

        @pl.when((slot == i) & (col != odd))
        def _():
            w01[...] = own[i][...]

        @pl.when((slot == i) & (col == odd))
        def _():
            w01[...] = sib[i][...]

    wr[col] = own[0][...]
    wr[1 - col] = sib[0][...]

    def gather(k, _):
        slot = jnp.where(odd == col, table[line + k], table[line + near + k])
        for i in range(count):

            @pl.when((slot == i) & (row > 1))
            def _():
                wg[k, col] = own[i][...]
                wg[k, 1 - col] = sib[i][...]

        return 0

    lax.fori_loop(0, owned, gather, 0)
    inverse = split(inv[...])
    cross = split(w01[...])

    @pl.when(odd == 0)
    def _():
        w01[...] = three(inverse, cross, 1, 0).T

    @pl.when(odd != 0)
    def _():
        w01[...] = three(cross, inverse, 1, 1)

    p01 = split(w01[...])
    solved = three(split(wr[0]), inverse, 1, 1)
    p0[...] = jnp.where(row == 0, lower_part(solved), solved)
    mine = split(p0[...])
    t1r[...] = wr[1] - three(mine, p01, 1, 1)
    for k in range(owned):
        tile_copy(k).wait()

    def body(k, _):
        @pl.when(row > 1)
        def _():
            g = three(split(wg[k, 0]), inverse, 1, 1)
            parts = split(g)
            t1g[k] = wg[k, 1] - three(parts, p01, 1, 1)
            acc[k] = acc[k] - three(mine, parts, 1, 1)

        @pl.when(row == 1)
        def _():
            g = split(three(inverse, split(above[k]), 1, 0))
            t1g[k] = (acc[k] - three(p01, g, 1, 0)).T
            acc[k] = acc[k] - three(mine, g, 1, 0)

        @pl.when(row == 0)
        def _():
            g = split(three(inverse, split(acc[k]), 1, 0))
            t1g[k] = jnp.zeros_like(acc[k])
            acc[k] = acc[k] - three(mine, g, 1, 0)

        return 0

    lax.fori_loop(0, owned, body, 0, unroll=2)


def late_kernel(owned, col_total, p0, t1r, t1g, acc, inv_own, inv_sib, out, inv, p1, res, sems):
    row, col, layer = place()

    @pl.when(col == 0)
    def _():
        unpack(inv_own, inv)

    @pl.when(col != 0)
    def _():
        unpack(inv_sib, inv)

    inverse = split(inv[...])
    solved = three(split(t1r[...]), inverse, 1, 1)
    solved = jnp.where(row == 1, lower_part(solved), solved)
    p1[...] = jnp.where(row == 0, 0.0, solved)
    mine = split(p1[...])

    def out_copy(k):
        return pltpu.make_async_copy(
            res.at[k], out.at[0, 0, :, k, 0, :], sems.at[k]
        )

    def body(k, _):
        block = (layer * owned + k) * col_total + col

        @pl.when(block == 0)
        def _():
            res[k] = p0[...]

        @pl.when(block == 1)
        def _():
            res[k] = p1[...]

        @pl.when(block > 1)
        def _():
            g = three(split(t1g[k]), inverse, 1, 1)
            res[k] = acc[k] - three(mine, split(g), 1, 1)

        out_copy(k).start()
        return 0

    lax.fori_loop(0, owned, body, 0, unroll=2)

    def end(k, _):
        out_copy(k).wait()
        return 0

    lax.fori_loop(0, owned, end, 0)


def call_early(dims, table, matrix, above, own, sib, inv_own, inv_sib):
    owned = dims[1]
    n = matrix.shape[2]
    block = jax.ShapeDtypeStruct((n, n), F32)
    stack = jax.ShapeDtypeStruct((owned, n, n), F32)
    return pl.pallas_call(
        functools.partial(early_kernel, dims),
        out_shape=(block, block, stack, stack),
        in_specs=[SMEM, HBM] + [VMEM] * (2 * len(own) + 3),
        out_specs=(VMEM,) * 4,
        scratch_shapes=[
            pltpu.VMEM((n, n), F32),
            pltpu.VMEM((n, n), F32),
            pltpu.VMEM((2, n, n), F32),
            pltpu.VMEM((owned, 2, n, n), F32),
            pltpu.SemaphoreType.DMA((owned,)),
        ],
        cost_estimate=pl.CostEstimate(flops=60 * n**3, transcendentals=0, bytes_accessed=32 * n * n * 4),
        compiler_params=grant(n, 2 * len(own) + 8 + 6 * owned),
        name="early",
    )(table, matrix, above, *own, *sib, inv_own, inv_sib)


def call_late(col_total, p0, t1r, t1g, acc, inv_own, inv_sib):
    owned, n, _ = acc.shape
    return pl.pallas_call(
        functools.partial(late_kernel, owned, col_total),
        out_shape=jax.ShapeDtypeStruct((1, 1, n, owned, 1, n), F32),
        in_specs=[VMEM] * 6,
        out_specs=ANY,
        scratch_shapes=[
            pltpu.VMEM((n, n), F32),
            pltpu.VMEM((n, n), F32),
            pltpu.VMEM((owned, n, n), F32),
            pltpu.SemaphoreType.DMA((owned,)),
        ],
        cost_estimate=pl.CostEstimate(flops=30 * n**3, transcendentals=0, bytes_accessed=16 * n * n * 4),
        compiler_params=grant(n, 6 + 3 * owned),
        name="late",
    )(p0, t1r, t1g, acc, inv_own, inv_sib)


def put(rounds, choices):
    for i, taken in enumerate(rounds):
        for k in range(len(choices)):
            pairs = choices[(i - 1 + k) % len(choices)]
            if i and all(s != a and t != b for s, t in pairs for a, b in taken):
                taken.extend(pairs)
                return i
    rounds.append(list(choices[(len(rounds) - 1) % len(choices)]))
    return len(rounds) - 1


def gather_plan(levels, near, layer_total, col_total):
    cores = range(col_total)
    rounds = [[((1, 1, l), (0, 0, l)) for l in range(layer_total)]]
    arrived = {}
    for l in range(layer_total):
        rounds[0] += [((y, 1 - y, l), (2 + y, 1 - y, l)) for y in range(2)]
        arrived[l, 1, "cross"] = 0
    for t in range(levels - 1, 1, -1):
        for l in range(layer_total):
            pairs = [((y, 1 - y, l), (2 * t + y, 1 - y, l)) for y in range(2)]
            arrived[l, t, "cross"] = put(rounds, [pairs])
    for l in range(layer_total):
        for gap in range(1, levels):
            for h in range(max(1, l * near), (l + 1) * near):
                for t in (h - gap, h + gap):
                    if 1 <= t < levels:
                        arrived[l, t, h] = put(
                            rounds,
                            [
                                [
                                    ((2 * h + y, c, (l + k) % layer_total), (2 * t + y, c, l))
                                    for y in range(2)
                                    for c in cores
                                ]
                                for k in range(layer_total)
                            ],
                        )
    return rounds, arrived


def pair_plan(levels, near, layer_total, count, arrived):
    plan = {}
    for l in range(layer_total):
        for t in range(levels):
            line = []
            for h in range(l * near, (l + 1) * near):
                if t == h and h > 0:
                    line.append((0, 0, h))
                elif (l, t, h) in arrived:
                    line.append((1, 1 + arrived[l, t, h], h))
            line.sort()
            step = {}
            for order, slot, h in line:
                j = max(0, slot - 2 - (count - 1 - near)) if order else 0
                while j in step:
                    j += 1
                step[j % near if j >= near else j] = (slot, h)
            plan[l, t] = step
    return plan


def on_device(matrix):
    row_total = lax.axis_size("row")
    col_total = lax.axis_size("col")
    layer_total = lax.axis_size("layer")
    col_blocks = matrix.shape[3]
    owned = col_blocks // layer_total
    levels = row_total // 2
    near = levels // layer_total
    swap = [(0, 1), (1, 0)]

    def device(r, c, l):
        return (r * col_total + c) * layer_total + l

    def permute(x, pairs):
        return lax.ppermute(x, AXES, [(device(*s), device(*t)) for s, t in pairs])

    def permute_rows(x, pairs, cores):
        return permute(
            x,
            [((a, c, l), (b, c, l)) for a, b in pairs for c in cores for l in range(layer_total)],
        )

    def sibling(x):
        return lax.ppermute(x, "col", swap)

    rounds, arrived = gather_plan(levels, near, layer_total, col_total)
    plan = pair_plan(levels, near, layer_total, len(rounds), arrived)
    first = [0]

    mine = matrix[0, 0, :, 0, 0, :]
    own = [mine]
    for pairs in rounds:
        own.append(permute(mine, pairs))
    other = sibling(mine)
    inv0, packed = call_first(mine)
    inv0_sib = permute(packed, [((0, 0, l), (0, 1, l)) for l in range(layer_total)])
    inv1, tiles = call_second(inv0, other, own[1], matrix, owned)
    above = permute(
        tiles,
        [((0, c, l), (1, c, l)) for c in range(col_total) for l in range(layer_total)],
    )

    sent = []
    for t in range(levels - 1, 0, -1):
        sent.append(permute_rows(inv1, [(0, 2 * t)], first))
    hop = permute_rows(inv1, [(0, 1)], first)

    for j in range(near):
        slots = {key: step[j][0] for key, step in plan.items() if j in step}
        used = sorted(set(slots.values()))
        pairs = []
        for l, t in slots:
            for c in range(col_total):
                pairs += [((2 * t + y, c, l), (2 * t + 1 - y, c, l)) for y in range(2)]
        send = call_pick(
            {key: used.index(slot) for key, slot in slots.items()},
            [own[slot] for slot in used],
        )
        own.append(permute(send, pairs))

    spread = []
    for t in range(levels - 1, 0, -1):
        spread.append(permute(inv0_sib, [((0, 1, l), (2 * t, 1, l)) for l in range(layer_total)]))
    even = sum(spread, inv0_sib)
    back = permute_rows(even, [(2 * t, 2 * t + 1) for t in range(levels)], [1])
    inv0_own = even + back
    inv0_sib = sibling(inv0_own)
    sib = [other]
    for x in own[1:]:
        sib.append(sibling(x))

    even = sum(sent, inv1)
    back = permute_rows(even, [(2 * t, 2 * t + 1) for t in range(1, levels)], first)
    table = []
    for l in range(layer_total):
        for t in range(levels):
            slots = {h: (slot, 1 + len(rounds) + j) for j, (slot, h) in plan[l, t].items()}
            near_rows = range(l * near, (l + 1) * near)
            table += [slots.get(h, (0, 0))[0] for h in near_rows]
            table += [slots.get(h, (0, 0))[1] for h in near_rows]
            table.append(1 + arrived[l, t, "cross"] if t else 0)
    dims = (len(own), owned, near, levels)
    p0, t1r, t1g, acc = call_early(
        dims, jnp.array(table, jnp.int32), matrix, above, own, sib, inv0_own, inv0_sib
    )
    even, hop, p0 = lax.optimization_barrier((even, hop, p0))
    inv1_own = even + hop + back
    inv1_sib = sibling(inv1_own)
    return call_late(col_total, p0, t1r, t1g, acc, inv1_own, inv1_sib)


def solution(mesh):
    in_specs = (P(None, "row", None, None, "col", None),)
    out_specs = P(None, "row", None, "layer", "col", None)
    levels = mesh.shape["row"] // 2
    near = levels // mesh.shape["layer"]
    _, _ = gather_plan(levels, near, mesh.shape["layer"], mesh.shape["col"])

    return jax.shard_map(
        on_device, mesh=mesh, in_specs=in_specs, out_specs=out_specs, check_vma=False
    )
```

```python
import functools

import jax
import jax.numpy as jnp
from jax import lax
from jax.experimental import pallas as pl
from jax.experimental.pallas import tpu as pltpu
from jax.sharding import PartitionSpec as P


HIGH = lax.Precision.HIGHEST
F32 = jnp.float32
AXES = ("row", "col", "layer")
VMEM = pl.BlockSpec(memory_space=pltpu.VMEM)
SMEM = pl.BlockSpec(memory_space=pltpu.SMEM)
ANY = pl.BlockSpec(memory_space=pl.ANY)
HBM = pl.BlockSpec(memory_space=pltpu.HBM)
LANES = 128
SUB = 8


def contract(left, right, ldim, rdim):
    return lax.dot_general(
        left,
        right,
        (((ldim,), (rdim,)), ((), ())),
        precision=HIGH,
        preferred_element_type=F32,
    )


def nn(a, b):
    return contract(a, b, 1, 0)


def tn(a, b):
    return contract(a, b, 0, 0)


def row_of(tile, k):
    return jnp.broadcast_to(tile[k : k + 1, :], tile.shape)


def lane_of(tile, lane):
    index = jnp.full(tile.shape, lane, jnp.int32)
    return jnp.take_along_axis(tile, index, axis=1)


def small_inverse(block):
    size = block.shape[0]
    tiles = size // SUB
    width = 2 * size
    rows = lax.broadcasted_iota(jnp.int32, (size, size), 0)
    cols = lax.broadcasted_iota(jnp.int32, (size, size), 1)
    eye = jnp.where(rows == cols, 1.0, 0.0).astype(F32)
    full = jnp.concatenate([block, eye], axis=1)
    v = [full[SUB * t : SUB * (t + 1)] for t in range(tiles)]
    sub = lax.broadcasted_iota(jnp.int32, (SUB, width), 0)
    for s in range(tiles):
        c = {(j, t): lane_of(v[t], SUB * s + j) for j in range(SUB) for t in range(s, tiles)}
        pivots = jnp.ones((SUB, width), F32)
        for k in range(0, SUB, 2):
            p = row_of(c[k, s], k)
            q = row_of(c[k, s], k + 1)
            w = row_of(c[k + 1, s], k + 1)
            det = p * w - q * q
            over_det = 1.0 / det
            over_p = 1.0 / p
            v0, v1 = row_of(v[s], k), row_of(v[s], k + 1)
            c0 = {j: row_of(c[j, s], k) for j in range(k + 2, SUB)}
            c1 = {j: row_of(c[j, s], k + 1) for j in range(k + 2, SUB)}
            pivots = jnp.where(sub == k, p, jnp.where(sub == k + 1, det * over_p, pivots))
            for t in range(s, tiles):
                m0 = w * c[k, t] - q * c[k + 1, t]
                m1 = p * c[k + 1, t] - q * c[k, t]
                for j in range(k + 2, SUB):
                    c[j, t] = c[j, t] - (m0 * c0[j] + m1 * c1[j]) * over_det
                if t == s:
                    m0 = jnp.where(
                        sub > k + 1, m0 * over_det, jnp.where(sub == k + 1, q * over_p, 0.0)
                    )
                    m1 = jnp.where(sub > k + 1, m1 * over_det, 0.0)
                    v[t] = v[t] - (m0 * v0 + m1 * v1)
                else:
                    v[t] = v[t] - (m0 * v0 + m1 * v1) * over_det
        v[s] = v[s] * lax.rsqrt(pivots)
    return jnp.concatenate(v, axis=0)[:, size:]


def inverse_factor(a, x):
    n = a.shape[0]
    base = min(n, LANES // 2)
    x[...] = jnp.zeros((n, n), F32)
    diagonal = a[:base, :base]
    for lo in range(0, n, base):
        hi, end = lo + base, lo + 2 * base
        inv = small_inverse(diagonal)
        if hi < n:
            upper = nn(inv, a[lo:hi, hi:end])
            diagonal = a[hi:end, hi:end] - tn(upper, upper)
        if lo:
            x[lo:hi, :lo] = nn(inv, x[lo:hi, :lo])
        x[lo:hi, lo:hi] = inv
        if hi < n:
            x[hi:end, :hi] = x[hi:end, :hi] - tn(upper, x[lo:hi, :hi])
        if end < n:
            rest = nn(inv, a[lo:hi, end:])
            a[hi:end, end:] = a[hi:end, end:] - tn(upper, rest)
            a[end:, end:] = a[end:, end:] - tn(rest, rest)
            x[end:, :hi] = x[end:, :hi] - tn(rest, x[lo:hi, :hi])


def split(x):
    high = x.astype(jnp.bfloat16)
    return high, (x - high.astype(F32)).astype(jnp.bfloat16)


def three(left, right, ldim, rdim):
    def part(a, b):
        return lax.dot_general(
            a, b, (((ldim,), (rdim,)), ((), ())), preferred_element_type=F32
        )

    return part(left[0], right[0]) + (part(left[0], right[1]) + part(left[1], right[0]))


def lower_part(x):
    rows = lax.broadcasted_iota(jnp.int32, x.shape, 0)
    cols = lax.broadcasted_iota(jnp.int32, x.shape, 1)
    return jnp.where(rows >= cols, x, 0.0)


def place():
    return lax.axis_index("row"), lax.axis_index("col"), lax.axis_index("layer")


def is_owner():
    row, col, _ = place()
    return (row == 0) & (col == 0)


def pack(x, out):
    n = x.shape[0]
    half, quarter = n // 2, n // 4
    out[:half] = x[half:]
    out[half:, :half] = x[:quarter, :half]
    out[half:, half:] = x[quarter:half, :half]


def unpack(source, x):
    n = x.shape[0]
    half, quarter = n // 2, n // 4
    x[half:] = source[:half]
    x[:quarter, :half] = source[half:, :half]
    x[quarter:half, :half] = source[half:, half:]
    x[:half, half:] = jnp.zeros((half, half), F32)


def first_kernel(w00, inv, packed, a):
    @pl.when(is_owner())
    def _():
        a[...] = w00[...]
        inverse_factor(a, inv)
        pack(inv, packed)

    @pl.when(jnp.logical_not(is_owner()))
    def _():
        packed[...] = jnp.zeros_like(packed)


def second_kernel(inv0, w01, w11, matrix, packed, tiles, a, x, sems):
    row, _, layer = place()
    owned = tiles.shape[0]

    def tile_copy(k):
        return pltpu.make_async_copy(
            matrix.at[0, 0, :, layer * owned + k, 0, :], tiles.at[k], sems.at[k]
        )

    @pl.when(row == 0)
    def _():
        for k in range(owned):
            tile_copy(k).start()

    @pl.when(is_owner())
    def _():
        q = nn(inv0[...], w01[...])
        a[...] = w11[...] - tn(q, q)
        inverse_factor(a, x)
        pack(x, packed)

    @pl.when(jnp.logical_not(is_owner()))
    def _():
        packed[...] = jnp.zeros_like(packed)

    @pl.when(row == 0)
    def _():
        for k in range(owned):
            tile_copy(k).wait()


def lookup(slots):
    row, _, layer = place()
    value = jnp.int32(0)
    for (l, t), slot in slots.items():
        value = jnp.where((layer == l) & (row // 2 == t), slot, value)
    return value


def pick_kernel(slots, *refs):
    *sources, out = refs
    slot = lookup(slots)
    for i, source in enumerate(sources):

        @pl.when(slot == i)
        def _():
            out[...] = source[...]


def grant(n, blocks):
    return pltpu.CompilerParams(vmem_limit_bytes=(blocks + 12) * n * n * 4)


def factor_cost(n):
    return pl.CostEstimate(flops=40 * n**3, transcendentals=0, bytes_accessed=64 * n * n * 4)


def call_first(w00):
    n = w00.shape[0]
    return pl.pallas_call(
        first_kernel,
        out_shape=(
            jax.ShapeDtypeStruct((n, n), F32),
            jax.ShapeDtypeStruct((n - n // 4, n), F32),
        ),
        in_specs=[VMEM],
        out_specs=(VMEM, VMEM),
        scratch_shapes=[pltpu.VMEM((n, n), F32)],
        cost_estimate=factor_cost(n),
        compiler_params=grant(n, 4),
        name="first",
    )(w00)


def call_second(inv0, w01, w11, matrix, owned):
    n = w11.shape[0]
    return pl.pallas_call(
        second_kernel,
        out_shape=(
            jax.ShapeDtypeStruct((n - n // 4, n), F32),
            jax.ShapeDtypeStruct((owned, n, n), F32),
        ),
        in_specs=[VMEM] * 3 + [HBM],
        out_specs=(VMEM, VMEM),
        scratch_shapes=[pltpu.VMEM((n, n), F32)] * 2 + [pltpu.SemaphoreType.DMA((owned,))],
        cost_estimate=factor_cost(n),
        compiler_params=grant(n, 6 + owned),
        name="second",
    )(inv0, w01, w11, matrix)


def call_pick(slots, sources):
    n = sources[0].shape[0]
    return pl.pallas_call(
        functools.partial(pick_kernel, slots),
        out_shape=jax.ShapeDtypeStruct((n, n), F32),
        in_specs=[VMEM] * len(sources),
        out_specs=VMEM,
        compiler_params=grant(n, 1 + len(sources)),
        name="pick",
    )(*sources)


def base_kernel(dims, table, *refs):
    count, near, levels = dims
    own, sib = refs[:count], refs[count : 2 * count]
    inv_own, inv_sib = refs[2 * count : 2 * count + 2]
    inv, p01, p0, t1r = refs[2 * count + 2 : 2 * count + 6]
    (wr,) = refs[2 * count + 6 :]
    row, col, layer = place()
    level, odd = row // 2, row % 2

    @pl.when(col == 1)
    def _():
        unpack(inv_own, inv)

    @pl.when(col != 1)
    def _():
        unpack(inv_sib, inv)

    slot = table[(layer * levels + level) * (2 * near + 1) + 2 * near]
    for i in range(count):

        @pl.when((slot == i) & (col != odd))
        def _():
            p01[...] = own[i][...]

        @pl.when((slot == i) & (col == odd))
        def _():
            p01[...] = sib[i][...]

    wr[col] = own[0][...]
    wr[1 - col] = sib[0][...]
    inverse = split(inv[...])
    cross = split(p01[...])

    @pl.when(odd == 0)
    def _():
        p01[...] = three(inverse, cross, 1, 0).T

    @pl.when(odd != 0)
    def _():
        p01[...] = three(cross, inverse, 1, 1)

    solved = three(split(wr[0]), inverse, 1, 1)
    p0[...] = jnp.where(row == 0, lower_part(solved), solved)
    t1r[...] = wr[1] - three(split(p0[...]), split(p01[...]), 1, 1)


def early_kernel(dims, table, matrix, above, inv, cross, panel, *refs):
    count, owned, near, levels = dims
    own, sib = refs[:count], refs[count : 2 * count]
    t1g, acc, wg, sems = refs[2 * count :]
    row, col, layer = place()
    level, odd = row // 2, row % 2

    def tile_copy(k):
        return pltpu.make_async_copy(
            matrix.at[0, 0, :, layer * owned + k, 0, :], acc.at[k], sems.at[k]
        )

    for k in range(owned):
        tile_copy(k).start()

    line = (layer * levels + level) * (2 * near + 1)

    def gather(k, _):
        slot = jnp.where(odd == col, table[line + k], table[line + near + k])
        for i in range(count):

            @pl.when((slot == i) & (row > 1))
            def _():
                wg[k, col] = own[i][...]
                wg[k, 1 - col] = sib[i][...]

        return 0

    lax.fori_loop(0, owned, gather, 0)
    inverse = split(inv[...])
    p01 = split(cross[...])
    mine = split(panel[...])
    for k in range(owned):
        tile_copy(k).wait()

    def body(k, _):
        @pl.when(row > 1)
        def _():
            g = three(split(wg[k, 0]), inverse, 1, 1)
            parts = split(g)
            t1g[k] = wg[k, 1] - three(parts, p01, 1, 1)
            acc[k] = acc[k] - three(mine, parts, 1, 1)

        @pl.when(row == 1)
        def _():
            g = split(three(inverse, split(above[k]), 1, 0))
            t1g[k] = (acc[k] - three(p01, g, 1, 0)).T
            acc[k] = acc[k] - three(mine, g, 1, 0)

        @pl.when(row == 0)
        def _():
            g = split(three(inverse, split(acc[k]), 1, 0))
            t1g[k] = jnp.zeros_like(acc[k])
            acc[k] = acc[k] - three(mine, g, 1, 0)

        return 0

    lax.fori_loop(0, owned, body, 0, unroll=2)


def late_kernel(owned, col_total, p0, t1r, t1g, acc, inv_own, inv_sib, out, inv, p1, res, sems):
    row, col, layer = place()

    @pl.when(col == 0)
    def _():
        unpack(inv_own, inv)

    @pl.when(col != 0)
    def _():
        unpack(inv_sib, inv)

    inverse = split(inv[...])
    solved = three(split(t1r[...]), inverse, 1, 1)
    solved = jnp.where(row == 1, lower_part(solved), solved)
    p1[...] = jnp.where(row == 0, 0.0, solved)
    mine = split(p1[...])

    def out_copy(k):
        return pltpu.make_async_copy(
            res.at[k], out.at[0, 0, :, k, 0, :], sems.at[k]
        )

    def body(k, _):
        block = (layer * owned + k) * col_total + col

        @pl.when(block == 0)
        def _():
            res[k] = p0[...]

        @pl.when(block == 1)
        def _():
            res[k] = p1[...]

        @pl.when(block > 1)
        def _():
            g = three(split(t1g[k]), inverse, 1, 1)
            res[k] = acc[k] - three(mine, split(g), 1, 1)

        out_copy(k).start()
        return 0

    lax.fori_loop(0, owned, body, 0, unroll=2)

    def end(k, _):
        out_copy(k).wait()
        return 0

    lax.fori_loop(0, owned, end, 0)


def call_base(dims, table, own, sib, inv_own, inv_sib):
    n = own[0].shape[0]
    block = jax.ShapeDtypeStruct((n, n), F32)
    return pl.pallas_call(
        functools.partial(base_kernel, dims),
        out_shape=(block,) * 4,
        in_specs=[SMEM] + [VMEM] * (2 * len(own) + 2),
        out_specs=(VMEM,) * 4,
        scratch_shapes=[pltpu.VMEM((2, n, n), F32)],
        cost_estimate=pl.CostEstimate(flops=20 * n**3, transcendentals=0, bytes_accessed=16 * n * n * 4),
        compiler_params=grant(n, 2 * len(own) + 8),
        name="base",
    )(table, *own, *sib, inv_own, inv_sib)


def call_early(dims, table, matrix, above, base, own, sib):
    owned = dims[1]
    n = matrix.shape[2]
    stack = jax.ShapeDtypeStruct((owned, n, n), F32)
    return pl.pallas_call(
        functools.partial(early_kernel, dims),
        out_shape=(stack, stack),
        in_specs=[SMEM, HBM] + [VMEM] * (2 * len(own) + 4),
        out_specs=(VMEM,) * 2,
        scratch_shapes=[
            pltpu.VMEM((owned, 2, n, n), F32),
            pltpu.SemaphoreType.DMA((owned,)),
        ],
        cost_estimate=pl.CostEstimate(flops=40 * n**3, transcendentals=0, bytes_accessed=32 * n * n * 4),
        compiler_params=grant(n, 2 * len(own) + 8 + 6 * owned),
        name="early",
    )(table, matrix, above, *base, *own, *sib)


def call_late(col_total, p0, t1r, t1g, acc, inv_own, inv_sib):
    owned, n, _ = acc.shape
    return pl.pallas_call(
        functools.partial(late_kernel, owned, col_total),
        out_shape=jax.ShapeDtypeStruct((1, 1, n, owned, 1, n), F32),
        in_specs=[VMEM] * 6,
        out_specs=ANY,
        scratch_shapes=[
            pltpu.VMEM((n, n), F32),
            pltpu.VMEM((n, n), F32),
            pltpu.VMEM((owned, n, n), F32),
            pltpu.SemaphoreType.DMA((owned,)),
        ],
        cost_estimate=pl.CostEstimate(flops=30 * n**3, transcendentals=0, bytes_accessed=16 * n * n * 4),
        compiler_params=grant(n, 6 + 3 * owned),
        name="late",
    )(p0, t1r, t1g, acc, inv_own, inv_sib)


def put(rounds, choices):
    for i, taken in enumerate(rounds):
        for k in range(len(choices)):
            pairs = choices[(i - 1 + k) % len(choices)]
            if i and all(s != a and t != b for s, t in pairs for a, b in taken):
                taken.extend(pairs)
                return i
    rounds.append(list(choices[(len(rounds) - 1) % len(choices)]))
    return len(rounds) - 1


def gather_plan(levels, near, layer_total, col_total):
    cores = range(col_total)
    rounds = [[((1, 1, l), (0, 0, l)) for l in range(layer_total)]]
    arrived = {}
    for l in range(layer_total):
        rounds[0] += [((y, 1 - y, l), (2 + y, 1 - y, l)) for y in range(2)]
        arrived[l, 1, "cross"] = 0
    for l in range(layer_total):
        for t in range(2, levels) if 2 * l < layer_total else range(levels - 1, 1, -1):
            pairs = [((y, 1 - y, l), (2 * t + y, 1 - y, l)) for y in range(2)]
            arrived[l, t, "cross"] = put(rounds, [pairs])
    for l in range(layer_total):
        for gap in range(1, levels):
            for h in range(max(1, l * near), (l + 1) * near):
                for t in (h - gap, h + gap):
                    if 1 <= t < levels:
                        arrived[l, t, h] = put(
                            rounds,
                            [
                                [
                                    ((2 * h + y, c, (l + k) % layer_total), (2 * t + y, c, l))
                                    for y in range(2)
                                    for c in cores
                                ]
                                for k in range(layer_total)
                            ],
                        )
    return rounds, arrived


def pair_plan(levels, near, layer_total, count, arrived):
    plan = {}
    for l in range(layer_total):
        for t in range(levels):
            line = []
            for h in range(l * near, (l + 1) * near):
                if t == h and h > 0:
                    line.append((0, 0, h))
                elif (l, t, h) in arrived:
                    line.append((1, 1 + arrived[l, t, h], h))
            line.sort()
            step = {}
            for order, slot, h in line:
                j = max(0, slot - 2 - (count - 1 - near)) if order else 0
                while j in step:
                    j += 1
                step[j % near if j >= near else j] = (slot, h)
            plan[l, t] = step
    return plan


def on_device(matrix):
    row_total = lax.axis_size("row")
    col_total = lax.axis_size("col")
    layer_total = lax.axis_size("layer")
    col_blocks = matrix.shape[3]
    owned = col_blocks // layer_total
    levels = row_total // 2
    near = levels // layer_total
    swap = [(0, 1), (1, 0)]

    def device(r, c, l):
        return (r * col_total + c) * layer_total + l

    def permute(x, pairs):
        return lax.ppermute(x, AXES, [(device(*s), device(*t)) for s, t in pairs])

    def permute_rows(x, pairs, cores):
        return permute(
            x,
            [((a, c, l), (b, c, l)) for a, b in pairs for c in cores for l in range(layer_total)],
        )

    def sibling(x):
        return lax.ppermute(x, "col", swap)

    rounds, arrived = gather_plan(levels, near, layer_total, col_total)
    plan = pair_plan(levels, near, layer_total, len(rounds), arrived)
    first = [0]

    mine = matrix[0, 0, :, 0, 0, :]
    own = [mine]
    for pairs in rounds:
        own.append(permute(mine, pairs))
    other = sibling(mine)
    inv0, packed = call_first(mine)
    inv0_sib = sibling(packed)
    inv1, tiles = call_second(inv0, other, own[1], matrix, owned)
    above = permute(
        tiles,
        [((0, c, l), (1, c, l)) for c in range(col_total) for l in range(layer_total)],
    )

    sent = []
    for t in range(levels - 1, 0, -1):
        sent.append(permute_rows(inv1, [(0, 2 * t)], first))
    hop = permute_rows(inv1, [(0, 1)], first)

    for j in range(near):
        slots = {key: step[j][0] for key, step in plan.items() if j in step}
        used = sorted(set(slots.values()))
        pairs = []
        for l, t in slots:
            for c in range(col_total):
                pairs += [((2 * t + y, c, l), (2 * t + 1 - y, c, l)) for y in range(2)]
        send = call_pick(
            {key: used.index(slot) for key, slot in slots.items()},
            [own[slot] for slot in used],
        )
        own.append(permute(send, pairs))

    spread = []
    for t in range(levels - 1, 0, -1):
        spread.append(permute(inv0_sib, [((0, 1, l), (2 * t, 1, l)) for l in range(layer_total)]))
    even = sum(spread, inv0_sib)
    back = permute_rows(even, [(2 * t, 2 * t + 1) for t in range(levels)], [1])
    inv0_own = even + back
    inv0_sib = sibling(inv0_own)
    sib = [other]
    for x in own[1:]:
        sib.append(sibling(x))

    even = sum(sent, inv1)
    back = permute_rows(even, [(2 * t, 2 * t + 1) for t in range(1, levels)], first)
    table = []
    for l in range(layer_total):
        for t in range(levels):
            slots = {h: (slot, 1 + len(rounds) + j) for j, (slot, h) in plan[l, t].items()}
            near_rows = range(l * near, (l + 1) * near)
            table += [slots.get(h, (0, 0))[0] for h in near_rows]
            table += [slots.get(h, (0, 0))[1] for h in near_rows]
            table.append(1 + arrived[l, t, "cross"] if t else 0)
    table = jnp.array(table, jnp.int32)
    raw = 1 + len(rounds)
    inv0_full, p01, p0, t1r = call_base(
        (raw, near, levels), table, own[:raw], sib[:raw], inv0_own, inv0_sib
    )
    dims = (len(own), owned, near, levels)
    t1g, acc = call_early(dims, table, matrix, above, (inv0_full, p01, p0), own, sib)
    even, hop, acc = lax.optimization_barrier((even, hop, acc))
    inv1_own = even + hop + back
    inv1_sib = sibling(inv1_own)
    return call_late(col_total, p0, t1r, t1g, acc, inv1_own, inv1_sib)


def solution(mesh):
    in_specs = (P(None, "row", None, None, "col", None),)
    out_specs = P(None, "row", None, "layer", "col", None)
    levels = mesh.shape["row"] // 2
    near = levels // mesh.shape["layer"]
    _, _ = gather_plan(levels, near, mesh.shape["layer"], mesh.shape["col"])

    return jax.shard_map(
        on_device, mesh=mesh, in_specs=in_specs, out_specs=out_specs, check_vma=False
    )
```
